512 devices in a mesh: tm: 64 (over z_hi, x, y), space: 8 (over z_lo, core).
Axes of the slice: x: 4, y: 8, z: 8 (z_hi: 2, z_lo: 4; z = z_hi * 4 + z_lo), core: 2. Of those that a mesh axis runs over, the one named last changes fastest.
Arguments:
- start_states: float32 [64, 128, 16, 128], P('tm', 'space'), may hold values from -6 to 6
- material: int32 [128, 16, 128], P('space'), may hold values from 0 to 15
- source: float32 [128, 16, 128], P('space'), may hold values from -0.6 to 0.6
- conductivity: float32 [16], replicated, may hold values from 0.02 to 0.16
- tide_amp: float32 [12], replicated, may hold values from -1.5 to 1.5
- phase: int32 [64], P('tm'), may hold values from 0 to 11
- coarse_rate: float32 [32, 4, 32], P('space'), may hold values from 0.3 to 40
Outputs:
- final_states: float32 [64, 128, 16, 128], P('tm', 'space')
The draws below stay inside these ranges and needn't reach their ends.
All inputs are finite; a program needn't handle non-finite values.
Results may differ from the reference program's by a relative error of at most 0.00013.
Values sent between devices are 32-bit elements; how exact they have to be, the bound alone decides.
A program may use at most 64 MiB of HBM per device.

```python
import math
import jax
import jax.numpy as jnp
from jax import lax

NX = 16
NY = 128
FINE = 10
ITERS = 2
CLASSES = 16
PHASES = 12
WINDOWS = 64
NZ = 128


def plant(entries, stream_key, smallest, top_value):
    longest = entries.shape.index(max(entries.shape))
    spots = []
    for shift in (0, 1):
        where = [jax.random.randint(jax.random.fold_in(stream_key, axis), (), 0, length) for axis, length in enumerate(entries.shape)]
        where[longest] = (where[longest] + shift) % entries.shape[longest]
        spots.append(tuple(where))
    return entries.at[spots[0]].set(smallest).at[spots[1]].set(top_value)


def steps_of(own_key, shape, cuts, low, largest):
    gain = 1.0
    for dim, shards_of in cuts:
        heights = jax.random.uniform(jax.random.fold_in(jax.random.fold_in(own_key, 6), dim), (shards_of,), jnp.float32, low / len(cuts), largest / len(cuts))
        gain = gain * jnp.repeat(jnp.exp(heights), shape[dim] // shards_of).reshape((-1,) + (1,) * (len(shape) - 1 - dim))
    return gain


def centred(key, extent, spread, reach, cuts=(), kind=jnp.bfloat16):
    loudness = steps_of(key, extent, cuts, -0.22, 0.18) if cuts else 1.0
    drawn = jax.random.normal(key, extent, jnp.float32) * spread * loudness
    return jnp.minimum(jnp.maximum(drawn, -reach), reach).astype(kind)


def setup_inputs(seed: int = 0) -> dict:
    splits = jax.random.split(jax.random.key(seed), 8)
    start_states = centred(splits[0], (WINDOWS, NZ, NX, NY), 1.0, 6.0, ((0, 64), (1, 8)), jnp.float32)
    material = plant(jax.random.randint(splits[1], (NZ, NX, NY), 0, CLASSES), jax.random.fold_in(splits[1], 1), 0, CLASSES - 1).astype(jnp.int32)
    source = centred(splits[2], (NZ, NX, NY), 0.1, 0.6, ((0, 8),), jnp.float32)
    conductivity = jnp.clip(jnp.exp(jax.random.uniform(splits[3], (CLASSES,), jnp.float32, math.log(0.02), math.log(0.16))), 0.02, 0.16)
    tide_amp = jnp.clip(jax.random.uniform(splits[4], (PHASES,), jnp.float32, -1.5, 1.5), -1.5, 1.5)
    phase = plant(jax.random.randint(splits[5], (WINDOWS,), 0, PHASES), jax.random.fold_in(splits[5], 1), 0, PHASES - 1).astype(jnp.int32)
    coarse_rate = jnp.clip(jnp.exp(math.log(40.0) - 4.8928522 * jax.random.uniform(splits[6], (NZ // 4, NX // 4, NY // 4), jnp.float32) ** steps_of(splits[6], (NZ // 4, NX // 4, NY // 4), ((0, 8),), -0.2, 0.2)), 0.3, 40.0)
    return dict(start_states=start_states, material=material, source=source, conductivity=conductivity, tide_amp=tide_amp, phase=phase, coarse_rate=coarse_rate)


def neighbour_total(field_now):
    framed = jnp.pad(field_now, 1)
    total = framed[2:, 1:-1, 1:-1] + framed[:-2, 1:-1, 1:-1]
    total = total + framed[1:-1, 2:, 1:-1] + framed[1:-1, :-2, 1:-1]
    total = total + framed[1:-1, 1:-1, 2:] + framed[1:-1, 1:-1, :-2]
    return total


def fine_sweeps(field_now, cell_coef, forcing):
    for substep in range(FINE):
        neighbours = neighbour_total(field_now)
        field_now = field_now + cell_coef * (neighbours - 6.0 * field_now) + forcing
    return field_now


def restrict(field_now):
    shape_all = field_now.shape
    lead = shape_all[:-3]
    depth, rows, cols = shape_all[-3:]
    blocks = field_now.reshape(lead + (depth // 4, 4, rows // 4, 4, cols // 4, 4))
    return blocks.mean(axis=(-5, -3, -1))


def prolong(coarse):
    shape_all = coarse.shape
    lead = shape_all[:-3]
    depth, rows, cols = shape_all[-3:]
    wide = jnp.broadcast_to(coarse[..., :, None, :, None, :, None], lead + (depth, 4, rows, 4, cols, 4))
    return wide.reshape(lead + (depth * 4, rows * 4, cols * 4))


def reference(start_states, material, source, conductivity, tide_amp, phase, coarse_rate):
    cell_coef = conductivity[material]
    levels = tide_amp[phase]
    decay = jnp.exp(-coarse_rate / WINDOWS)
    closure = 1.0 - jnp.exp(-coarse_rate)
    counts = jnp.arange(WINDOWS).astype(jnp.float32)
    powers = jnp.exp(-coarse_rate[None] * counts[:, None, None, None] / WINDOWS)
    states = start_states
    for outer in range(ITERS):
        ends = lax.map(lambda pair: fine_sweeps(pair[0], cell_coef, pair[1] * source), (states, levels))
        coarse_start = restrict(states)
        jumps = restrict(ends) - decay[None] * coarse_start

        def advance(running, jump_now):
            return decay * running + jump_now, running

        loop_total, prefixes = lax.scan(advance, jnp.zeros_like(decay), jumps)
        coarse = powers * (loop_total / closure)[None] + prefixes
        corrected = ends + prolong(decay[None] * (coarse - coarse_start))
        states = jnp.roll(corrected, 1, axis=0)
    return states
```

```python
import jax
import jax.numpy as jnp
from jax import lax
from jax.experimental import pallas as pl
from jax.experimental.pallas import tpu as pltpu
from jax.sharding import PartitionSpec as P

FINE = 10
WINDOWS = 64
SLABS = 8
LAYERS = 16
HALO = FINE
EXT = LAYERS + 2 * HALO
MESH = pl.DeviceIdType.MESH
GROUPS = ((1, 3), (4, 3), (7, 4))


def roll(x, shift, axis):
    return pltpu.roll(x, shift % x.shape[axis], axis)


def make_kernel():
    def kernel(
        start, material, source, cond, amp, phase, rate, out,
        nat_u, nat_m, nat_s, u, coef, force, src, level, jbuf, kbuf, ksend,
        weight, cown, cghost, dhalo, fin,
        loc_sem, h_send, h_recv, j_send, j_recv, k_send, k_recv,
        d_send, d_recv, c_send, c_recv, l_send, l_recv, f_send, f_recv,
    ):
        tm = lax.axis_index("tm")
        slab = lax.axis_index("space")
        yy = lax.rem(tm, 8)
        group = tm // 8
        xx = lax.rem(group, 4)
        zz = group // 4
        has_low = slab > 0
        has_high = slab < SLABS - 1

        def y_peer(j):
            return (group * 8 + lax.rem(yy + j, 8), slab)

        def g_index(dz, dx):
            return lax.rem(zz + dz, 2) * 4 + lax.rem(xx + dx, 4)

        def g_peer(dz, dx):
            return (g_index(dz, dx) * 8 + yy, slab)

        def t_peer(shift):
            return (lax.rem(tm + shift + WINDOWS, WINDOWS), slab)

        own = pl.ds(HALO, LAYERS)
        locals_ = [
            pltpu.make_async_copy(start.at[0], nat_u.at[own], loc_sem.at[0]),
            pltpu.make_async_copy(material, nat_m.at[own], loc_sem.at[1]),
            pltpu.make_async_copy(source, nat_s.at[own], loc_sem.at[2]),
        ]
        for copy in locals_:
            copy.start()

        barrier = pltpu.get_barrier_semaphore()

        def greet(peer):
            pl.semaphore_signal(barrier, inc=1, device_id=peer, device_id_type=MESH)

        @pl.when(has_low)
        def _():
            greet((tm, slab - 1))

        @pl.when(has_high)
        def _():
            greet((tm, slab + 1))

        for j in range(1, 8):
            greet(y_peer(j))
        pairs = [(dz, dx) for dz in (1, 0) for dx in (2, 1, 3, 0) if (dz, dx) != (0, 0)]
        for dz, dx in pairs:
            greet(g_peer(dz, dx))
        for shift in (1, -1, 2, -2):
            greet(t_peer(shift))

        level_own = amp[phase[0]]
        level[0] = jnp.full((8, 128), level_own, jnp.float32)

        sides = jnp.where(has_low, 1, 0) + jnp.where(has_high, 1, 0)
        pl.semaphore_wait(barrier, 18 + sides)

        def halo_copies(side):
            peer = (tm, slab - 1) if side == 0 else (tm, slab + 1)
            rows = pl.ds(0, HALO) if side == 0 else pl.ds(LAYERS - HALO, HALO)
            ghost = pl.ds(HALO + LAYERS, HALO) if side == 0 else pl.ds(0, HALO)
            sources = (start.at[0, rows], material.at[rows], source.at[rows])
            targets = (nat_u.at[ghost], nat_m.at[ghost], nat_s.at[ghost])
            return [
                pltpu.make_async_remote_copy(
                    src_ref=a, dst_ref=b, send_sem=h_send.at[side, i],
                    recv_sem=h_recv.at[side, i], device_id=peer, device_id_type=MESH,
                )
                for i, (a, b) in enumerate(zip(sources, targets))
            ]

        @pl.when(has_high)
        def _():
            for copy in halo_copies(1):
                copy.start()

        @pl.when(has_low)
        def _():
            for copy in halo_copies(0):
                copy.start()

        level_copy = pltpu.make_async_remote_copy(
            src_ref=level.at[0], dst_ref=level.at[1], send_sem=l_send,
            recv_sem=l_recv, device_id=t_peer(-1), device_id_type=MESH,
        )
        level_copy.start()

        sub = lax.broadcasted_iota(jnp.int32, (8, 128), 0)
        lane = lax.broadcasted_iota(jnp.int32, (8, 128), 1)
        first_lane, last_lane = lane == 0, lane == 127
        first_sub, last_sub = sub == 0, sub == 7
        even_sub, even_lane = (sub & 1) == 0, (lane & 1) == 0
        low_pair = (lane & 3) < 2
        owner = (sub >> 1) == (lane & 3)
        pick = sub == 2 * (lane & 3)
        zero = jnp.zeros((8, 128), jnp.float32)

        def lane_total(x):
            x = x + jnp.where(even_lane, roll(x, -1, 1), roll(x, 1, 1))
            return x + jnp.where(low_pair, roll(x, -2, 1), roll(x, 2, 1))

        def block_mean(layers):
            total = layers[0]
            for part in layers[1:]:
                total = total + part
            total = total + jnp.where(even_sub, roll(total, -1, 0), roll(total, 1, 0))
            return lane_total(total) * (1.0 / 64.0)

        def pack(means):
            rows = [
                jnp.sum(jnp.where(pick, m, zero), axis=0, keepdims=True) for m in means
            ]
            return jnp.concatenate(rows, axis=0)

        def unpack(row):
            wide = jnp.broadcast_to(row, (8, 128))
            return lane_total(jnp.where(owner, wide, zero))

        def clear(side):
            def go(i, _):
                k = i + (HALO + LAYERS if side else 0)
                nat_u[k] = jnp.zeros((16, 128), jnp.float32)
                nat_s[k] = jnp.zeros((16, 128), jnp.float32)
                nat_m[k] = jnp.zeros((16, 128), jnp.int32)
                dhalo[side, i] = jnp.zeros((2, 8, 128), jnp.float32)
                return 0

            lax.fori_loop(0, HALO, go, 0)
            cghost[side] = jnp.zeros((4, 128), jnp.float32)

        @pl.when(jnp.logical_not(has_low))
        def _():
            clear(0)

        @pl.when(jnp.logical_not(has_high))
        def _():
            clear(1)

        spread_row = lax.broadcasted_iota(jnp.int32, (32, 128), 0)
        spread_col = lax.broadcasted_iota(jnp.int32, (32, 128), 1)
        spread = jnp.where(spread_row == (spread_col >> 2), 1.0, 0.0).astype(jnp.float32)
        quarter = lax.broadcasted_iota(jnp.int32, (4, 128), 0) == (
            lax.broadcasted_iota(jnp.int32, (4, 128), 1) & 3
        )
        rows = []
        for zc in range(4):
            wide = jnp.dot(
                rate[zc], spread, precision=lax.Precision.HIGHEST,
                preferred_element_type=jnp.float32,
            )
            rows.append(jnp.sum(jnp.where(quarter, wide, 0.0), axis=0, keepdims=True))
        packed_rate = jnp.concatenate(rows, axis=0)
        step_rate = packed_rate * (-1.0 / WINDOWS)
        decay = jnp.exp(step_rate)
        unclose = 1.0 / (1.0 - jnp.exp(-packed_rate))

        def powers(i, _):
            weight[i] = jnp.exp(step_rate * i.astype(jnp.float32))
            return 0

        lax.fori_loop(0, WINDOWS, powers, 0)

        def lookup(m):
            picks = [cond[i] for i in range(16)]
            for bit in range(4):
                on = (m & (1 << bit)) != 0
                picks = [
                    jnp.where(on, picks[2 * i + 1], picks[2 * i])
                    for i in range(len(picks) // 2)
                ]
            return picks[0]

        level1 = level[0]

        def arrange(lo, count, gain):
            def go(i, _):
                for half in range(2):
                    rows = pl.ds(half, 8, stride=2)
                    k = lo + i
                    u[k, half] = nat_u[k, rows, :]
                    c = lookup(nat_m[k, rows, :])
                    coef[k, half] = c if gain is None else c * gain
                    s = nat_s[k, rows, :]
                    src[k, half] = s
                    force[k, half] = level1 * s
                return 0

            lax.fori_loop(0, count, go, 0, unroll=2)

        for copy in locals_:
            copy.wait()
        arrange(HALO, LAYERS, None)

        def slab_means():
            means = []
            for zc in range(4):
                base = HALO + 4 * zc
                means.append(
                    block_mean([u[base + i, half] for i in range(4) for half in range(2)])
                )
            return means

        start_mean = pack(slab_means())

        @pl.when(has_low)
        def _():
            for copy in halo_copies(1):
                copy.wait_recv()

        @pl.when(has_high)
        def _():
            for copy in halo_copies(0):
                copy.wait_recv()

        arrange(0, HALO, jnp.where(has_low, 1.0, 0.0))
        arrange(HALO + LAYERS, HALO, jnp.where(has_high, 1.0, 0.0))

        def sweep(lo, hi):
            before = (u[lo - 1, 0], u[lo - 1, 1])
            here = (u[lo, 0], u[lo, 1])
            for k in range(lo, hi):
                after = (u[k + 1, 0], u[k + 1, 1])
                even, odd = here
                across = (
                    odd + jnp.where(first_sub, zero, roll(odd, 1, 0)),
                    even + jnp.where(last_sub, zero, roll(even, -1, 0)),
                )
                for half in range(2):
                    now = here[half]
                    total = before[half] + after[half] + across[half]
                    total = total + jnp.where(first_lane, zero, roll(now, 1, 1))
                    total = total + jnp.where(last_lane, zero, roll(now, -1, 1))
                    u[k, half] = now + coef[k, half] * (total - 6.0 * now) + force[k, half]
                before, here = here, after

        def fine():
            for first, count in GROUPS:
                def go(i, _):
                    sweep(first, EXT - first)
                    return 0

                lax.fori_loop(0, count, go, 0)

        def coarse_solve(it, jump, offset, between):
            jbuf[it, 0] = jump
            sends = []
            for j in (4, 3, 5, 2, 6, 1, 7):
                copy = pltpu.make_async_remote_copy(
                    src_ref=jbuf.at[it, 0], dst_ref=jbuf.at[it, j],
                    send_sem=j_send.at[it, j], recv_sem=j_recv.at[it, j],
                    device_id=y_peer(j), device_id_type=MESH,
                )
                copy.start()
                sends.append(copy)
            between()
            for copy in sends:
                copy.wait_recv()
            jumps = [jbuf[it, j] for j in range(8)]

            def partial(target_group):
                total = None
                for j in range(8):
                    origin = group * 8 + lax.rem(yy - j + 8, 8)
                    lag = lax.rem(target_group * 8 + yy - offset - origin + 2 * WINDOWS, WINDOWS)
                    term = weight[lag] * jumps[j]
                    total = term if total is None else total + term
                return total

            for dz, dx in pairs:
                slot = dz * 4 + dx
                ksend[it, slot] = partial(g_index(dz, dx))
                copy = pltpu.make_async_remote_copy(
                    src_ref=ksend.at[it, slot], dst_ref=kbuf.at[it, slot],
                    send_sem=k_send.at[it, slot], recv_sem=k_recv.at[it, slot],
                    device_id=g_peer(dz, dx), device_id_type=MESH,
                )
                copy.start()
                sends.append(copy)
            total = partial(group)
            for copy in sends[7:]:
                copy.wait_recv()
            for dz, dx in pairs:
                total = total + kbuf[it, dz * 4 + dx]
            return total * unclose, sends

        pending = []
        fine()

        def detach():
            means = slab_means()
            for zc in range(4):
                for i in range(4):
                    k = HALO + 4 * zc + i
                    for half in range(2):
                        u[k, half] = u[k, half] - means[zc]
            return pack(means)

        end_mean = detach()
        jump = end_mean - decay * start_mean

        def halo2(side):
            peer = (tm, slab - 1) if side == 0 else (tm, slab + 1)
            rows = pl.ds(HALO, HALO) if side == 0 else pl.ds(LAYERS, HALO)
            return pltpu.make_async_remote_copy(
                src_ref=u.at[rows], dst_ref=dhalo.at[1 - side],
                send_sem=d_send.at[side], recv_sem=d_recv.at[side],
                device_id=peer, device_id_type=MESH,
            )

        def ghost_mean(side):
            peer = (tm, slab - 1) if side == 0 else (tm, slab + 1)
            return pltpu.make_async_remote_copy(
                src_ref=cown, dst_ref=cghost.at[1 - side],
                send_sem=c_send.at[side], recv_sem=c_recv.at[side],
                device_id=peer, device_id_type=MESH,
            )

        def between1():
            @pl.when(has_high)
            def _():
                halo2(1).start()

            @pl.when(has_low)
            def _():
                halo2(0).start()

            level_copy.wait_recv()
            level2 = level[1]

            def go(k, _):
                for half in range(2):
                    force[k, half] = level2 * src[k, half]
                return 0

            lax.fori_loop(0, EXT, go, 0, unroll=4)

        coarse, sends = coarse_solve(0, jump, 0, between1)
        pending += sends
        cown[...] = coarse

        @pl.when(has_high)
        def _():
            ghost_mean(1).start()
            halo2(1).wait_send()

        @pl.when(has_low)
        def _():
            ghost_mean(0).start()
            halo2(0).wait_send()

        for zc in range(4):
            wide = unpack(coarse[zc:zc + 1])
            for i in range(4):
                k = HALO + 4 * zc + i
                for half in range(2):
                    u[k, half] = u[k, half] + wide

        @pl.when(has_low)
        def _():
            halo2(1).wait_recv()
            ghost_mean(1).wait_recv()

        @pl.when(has_high)
        def _():
            halo2(0).wait_recv()
            ghost_mean(0).wait_recv()

        low_wide = {r: unpack(cghost[0, r:r + 1, :]) for r in (1, 2, 3)}
        high_wide = {r: unpack(cghost[1, r:r + 1, :]) for r in (0, 1, 2)}
        for i in range(HALO):
            for half in range(2):
                u[i, half] = dhalo[0, i, half] + low_wide[(LAYERS - HALO + i) // 4]
                u[HALO + LAYERS + i, half] = dhalo[1, i, half] + high_wide[i // 4]

        fine()

        end_mean = detach()
        jump = end_mean - decay * coarse
        final_copy = pltpu.make_async_remote_copy(
            src_ref=u.at[own], dst_ref=fin, send_sem=f_send, recv_sem=f_recv,
            device_id=t_peer(2), device_id_type=MESH,
        )
        coarse, sends = coarse_solve(1, jump, 2, final_copy.start)
        pending += sends
        wides = [unpack(coarse[zc:zc + 1]) for zc in range(4)]
        final_copy.wait_recv()
        for zc in range(4):
            for i in range(4):
                k = 4 * zc + i
                for half in range(2):
                    out[0, k, pl.ds(half, 8, stride=2), :] = fin[k, half] + wides[zc]

        for copy in pending:
            copy.wait_send()
        final_copy.wait_send()
        level_copy.wait_send()

        @pl.when(has_high)
        def _():
            for copy in halo_copies(1):
                copy.wait_send()
            ghost_mean(1).wait_send()

        @pl.when(has_low)
        def _():
            for copy in halo_copies(0):
                copy.wait_send()
            ghost_mean(0).wait_send()

    return kernel


def body(start_states, material, source, conductivity, tide_amp, phase, coarse_rate):
    f32 = jnp.float32
    smem = pl.BlockSpec(memory_space=pltpu.SMEM)
    hbm = pl.BlockSpec(memory_space=pl.ANY)
    vmem = pl.BlockSpec(memory_space=pltpu.VMEM)
    dma = pltpu.SemaphoreType.DMA
    field = pltpu.VMEM((EXT, 2, 8, 128), f32)
    return pl.pallas_call(
        make_kernel(),
        out_shape=jax.ShapeDtypeStruct((1, LAYERS, 16, 128), f32),
        in_specs=[hbm, hbm, hbm, smem, smem, smem, vmem],
        out_specs=vmem,
        scratch_shapes=[
            pltpu.VMEM((EXT, 16, 128), f32),
            pltpu.VMEM((EXT, 16, 128), jnp.int32),
            pltpu.VMEM((EXT, 16, 128), f32),
            field, field, field, field,
            pltpu.VMEM((2, 8, 128), f32),
            pltpu.VMEM((2, 8, 4, 128), f32),
            pltpu.VMEM((2, 8, 4, 128), f32),
            pltpu.VMEM((2, 8, 4, 128), f32),
            pltpu.VMEM((WINDOWS, 4, 128), f32),
            pltpu.VMEM((4, 128), f32),
            pltpu.VMEM((2, 4, 128), f32),
            pltpu.VMEM((2, HALO, 2, 8, 128), f32),
            pltpu.VMEM((LAYERS, 2, 8, 128), f32),
            dma((3,)), dma((2, 3)), dma((2, 3)),
            dma((2, 8)), dma((2, 8)), dma((2, 8)), dma((2, 8)),
            dma((2,)), dma((2,)), dma((2,)), dma((2,)),
            dma(()), dma(()), dma(()), dma(()),
        ],
        compiler_params=pltpu.CompilerParams(collective_id=0, has_side_effects=True),
    )(start_states, material, source, conductivity, tide_amp, phase, coarse_rate)


def solution(mesh):
    placed = (
        P("tm", "space", None, None),
        P("space", None, None),
        P("space", None, None),
        P(),
        P(),
        P("tm"),
        P("space", None, None),
    )
    return jax.shard_map(
        body, mesh=mesh, in_specs=placed, out_specs=P("tm", "space", None, None), check_vma=False
    )
```

```python
import jax
import jax.numpy as jnp
from jax import lax
from jax.experimental import pallas as pl
from jax.experimental.pallas import tpu as pltpu
from jax.sharding import PartitionSpec as P

FINE = 10
WINDOWS = 64
SLABS = 8
LAYERS = 16
HALO = FINE
EXT = LAYERS + 2 * HALO
MESH = pl.DeviceIdType.MESH
GROUPS = ((1, 3), (4, 3), (7, 4))


def roll(x, shift, axis):
    return pltpu.roll(x, shift % x.shape[axis], axis)


def make_kernel():
    def kernel(
        start, material, source, cond, amp, phase, rate, out,
        nat_u, nat_m, nat_s, u, coef, force, src, jbuf, ksend, kbuf, tsend,
        ghost, weight, dhalo, fin,
        loc_sem, h_send, h_recv, j_send, j_recv, k_send, k_recv,
        d_send, d_recv, g_send, g_recv, f_send, f_recv, near, ring, cross, up,
    ):
        tm = lax.axis_index("tm")
        slab = lax.axis_index("space")
        yy = lax.rem(tm, 8)
        group = tm // 8
        xx = lax.rem(group, 4)
        zz = group // 4
        has_low = slab > 0
        has_high = slab < SLABS - 1

        def plane_peer(dx, dy):
            x, y = lax.rem(xx + dx, 4), lax.rem(yy + dy, 8)
            return ((zz * 4 + x) * 8 + y, slab)

        twin_tm = lax.rem(tm + 32, WINDOWS)
        twin = (twin_tm, slab)
        last = lax.rem(tm + 2, WINDOWS)

        own = pl.ds(HALO, LAYERS)
        locals_ = [
            pltpu.make_async_copy(start.at[0], nat_u.at[own], loc_sem.at[0]),
            pltpu.make_async_copy(material, nat_m.at[own], loc_sem.at[1]),
            pltpu.make_async_copy(source, nat_s.at[own], loc_sem.at[2]),
        ]
        for copy in locals_:
            copy.start()

        barrier = pltpu.get_barrier_semaphore()

        def greet(peer):
            pl.semaphore_signal(barrier, inc=1, device_id=peer, device_id_type=MESH)

        @pl.when(has_low)
        def _():
            greet((tm, slab - 1))

        @pl.when(has_high)
        def _():
            greet((tm, slab + 1))

        for dx, dy in ((0, 1), (0, 7), (1, 0), (3, 0)):
            greet(plane_peer(dx, dy))

        @pl.when(zz == 0)
        def _():
            greet(twin)

        def tell(sem, peers):
            for peer in peers:
                pl.semaphore_signal(sem, inc=1, device_id=peer, device_id_type=MESH)

        level_own = amp[phase[0]]
        jbuf[0, 0, 4:8, :] = jnp.full((4, 128), level_own, jnp.float32)

        sides = jnp.where(has_low, 1, 0) + jnp.where(has_high, 1, 0)
        pl.semaphore_wait(barrier, 4 + sides + zz)

        def halo_copies(side):
            peer = (tm, slab - 1) if side == 0 else (tm, slab + 1)
            rows = pl.ds(0, HALO) if side == 0 else pl.ds(LAYERS - HALO, HALO)
            ghost = pl.ds(HALO + LAYERS, HALO) if side == 0 else pl.ds(0, HALO)
            sources = (start.at[0, rows], material.at[rows], source.at[rows])
            targets = (nat_u.at[ghost], nat_m.at[ghost], nat_s.at[ghost])
            return [
                pltpu.make_async_remote_copy(
                    src_ref=a, dst_ref=b, send_sem=h_send.at[side, i],
                    recv_sem=h_recv.at[side, i], device_id=peer, device_id_type=MESH,
                )
                for i, (a, b) in enumerate(zip(sources, targets))
            ]

        @pl.when(has_high)
        def _():
            for copy in halo_copies(1):
                copy.start()

        @pl.when(has_low)
        def _():
            for copy in halo_copies(0):
                copy.start()

        @pl.when(zz == 1)
        def _():
            tell(up, (twin,))

        around = tuple(plane_peer(dx, dy) for dx, dy in ((0, 1), (0, 7), (1, 0), (3, 0)))
        tell(near, around)

        sub = lax.broadcasted_iota(jnp.int32, (8, 128), 0)
        lane = lax.broadcasted_iota(jnp.int32, (8, 128), 1)
        first_lane, last_lane = lane == 0, lane == 127
        first_sub, last_sub = sub == 0, sub == 7
        even_sub, even_lane = (sub & 1) == 0, (lane & 1) == 0
        low_pair = (lane & 3) < 2
        owner = (sub >> 1) == (lane & 3)
        pick = sub == 2 * (lane & 3)
        zero = jnp.zeros((8, 128), jnp.float32)

        def lane_total(x):
            x = x + jnp.where(even_lane, roll(x, -1, 1), roll(x, 1, 1))
            return x + jnp.where(low_pair, roll(x, -2, 1), roll(x, 2, 1))

        def block_mean(layers):
            total = layers[0]
            for part in layers[1:]:
                total = total + part
            total = total + jnp.where(even_sub, roll(total, -1, 0), roll(total, 1, 0))
            return lane_total(total) * (1.0 / 64.0)

        def pack(means):
            rows = [
                jnp.sum(jnp.where(pick, m, zero), axis=0, keepdims=True) for m in means
            ]
            return jnp.concatenate(rows, axis=0)

        def unpack(row):
            wide = jnp.broadcast_to(row, (8, 128))
            return lane_total(jnp.where(owner, wide, zero))

        def clear(side):
            def go(i, _):
                k = i + (HALO + LAYERS if side else 0)
                nat_u[k] = jnp.zeros((16, 128), jnp.float32)
                nat_s[k] = jnp.zeros((16, 128), jnp.float32)
                nat_m[k] = jnp.zeros((16, 128), jnp.int32)
                dhalo[side, i] = jnp.zeros((2, 8, 128), jnp.float32)
                return 0

            lax.fori_loop(0, HALO, go, 0)
            for part in range(2):
                ghost[part, side] = jnp.zeros((4, 128), jnp.float32)

        @pl.when(jnp.logical_not(has_low))
        def _():
            clear(0)

        @pl.when(jnp.logical_not(has_high))
        def _():
            clear(1)

        spread_row = lax.broadcasted_iota(jnp.int32, (32, 128), 0)
        spread_col = lax.broadcasted_iota(jnp.int32, (32, 128), 1)
        spread = jnp.where(spread_row == (spread_col >> 2), 1.0, 0.0).astype(jnp.float32)
        quarter = lax.broadcasted_iota(jnp.int32, (4, 128), 0) == (
            lax.broadcasted_iota(jnp.int32, (4, 128), 1) & 3
        )
        rows = []
        for zc in range(4):
            wide = jnp.dot(
                rate[zc], spread, precision=lax.Precision.HIGHEST,
                preferred_element_type=jnp.float32,
            )
            rows.append(jnp.sum(jnp.where(quarter, wide, 0.0), axis=0, keepdims=True))
        packed_rate = jnp.concatenate(rows, axis=0)
        step_rate = packed_rate * (-1.0 / WINDOWS)
        decay = jnp.exp(step_rate)
        unclose = 1.0 / (1.0 - jnp.exp(-packed_rate))

        def powers(it):
            def go(i, _):
                dx, dy = i // 8, lax.rem(i, 8)
                lag = (xx - lax.rem(xx - dx + 4, 4)) * 8 + yy - lax.rem(yy - dy + 8, 8)
                for half in range(2):
                    power = lax.rem(lag - 2 * it + 32 * half + 2 * WINDOWS, WINDOWS)
                    weight[it, half, i] = jnp.exp(step_rate * power.astype(jnp.float32)) * unclose
                return 0

            lax.fori_loop(0, 32, go, 0, unroll=2)

        powers(0)

        def lookup(m):
            picks = [cond[i] for i in range(16)]
            for bit in range(4):
                on = (m & (1 << bit)) != 0
                picks = [
                    jnp.where(on, picks[2 * i + 1], picks[2 * i])
                    for i in range(len(picks) // 2)
                ]
            return picks[0]

        level1 = level_own

        def arrange(lo, count, gain):
            def go(i, _):
                for half in range(2):
                    rows = pl.ds(half, 8, stride=2)
                    k = lo + i
                    u[k, half] = nat_u[k, rows, :]
                    c = lookup(nat_m[k, rows, :])
                    coef[k, half] = c if gain is None else c * gain
                    s = nat_s[k, rows, :]
                    src[k, half] = s
                    force[k, half] = level1 * s
                return 0

            lax.fori_loop(0, count, go, 0, unroll=2)

        pl.semaphore_wait(near, 4)
        tell(ring, tuple(plane_peer(dx, dy) for dx, dy in ((0, 2), (0, 6), (1, 0), (3, 0))))
        for copy in locals_:
            copy.wait()
        arrange(HALO, LAYERS, None)

        def slab_means():
            means = []
            for zc in range(4):
                base = HALO + 4 * zc
                means.append(
                    block_mean([u[base + i, half] for i in range(4) for half in range(2)])
                )
            return means

        start_mean = pack(slab_means())

        @pl.when(has_low)
        def _():
            for copy in halo_copies(1):
                copy.wait_recv()

        @pl.when(has_high)
        def _():
            for copy in halo_copies(0):
                copy.wait_recv()

        arrange(0, HALO, jnp.where(has_low, 1.0, 0.0))
        arrange(HALO + LAYERS, HALO, jnp.where(has_high, 1.0, 0.0))

        def sweep(lo, hi):
            before = (u[lo - 1, 0], u[lo - 1, 1])
            here = (u[lo, 0], u[lo, 1])
            for k in range(lo, hi):
                after = (u[k + 1, 0], u[k + 1, 1])
                even, odd = here
                across = (
                    odd + jnp.where(first_sub, zero, roll(odd, 1, 0)),
                    even + jnp.where(last_sub, zero, roll(even, -1, 0)),
                )
                for half in range(2):
                    now = here[half]
                    total = before[half] + after[half] + across[half]
                    total = total + jnp.where(first_lane, zero, roll(now, 1, 1))
                    total = total + jnp.where(last_lane, zero, roll(now, -1, 1))
                    u[k, half] = now + coef[k, half] * (total - 6.0 * now) + force[k, half]
                before, here = here, after

        def fine():
            for first, count in GROUPS:
                def go(i, _):
                    sweep(first, EXT - first)
                    return 0

                lax.fori_loop(0, count, go, 0)

        def coarse_solve(it, jump, between):
            rows = pl.ds(0, 8 if it == 0 else 4)
            jbuf[it, 0, 0:4, :] = jump
            sends = []
            for dx, dy in peers:
                slot = 8 * dx + dy
                copy = pltpu.make_async_remote_copy(
                    src_ref=jbuf.at[it, 0, rows], dst_ref=jbuf.at[it, slot, rows],
                    send_sem=j_send.at[it, slot], recv_sem=j_recv.at[it, slot],
                    device_id=plane_peer(dx, dy), device_id_type=MESH,
                )
                copy.start()
                sends.append(copy)
            between()
            for copy in sends:
                copy.wait_recv()

            def weigh(half):
                terms = [weight[it, half, i] * jbuf[it, i, 0:4, :] for i in range(32)]
                while len(terms) > 1:
                    terms = [a + b for a, b in zip(terms[::2], terms[1::2])]
                return terms[0]

            ksend[it, 0:4, :] = weigh(1)
            if it == 0:
                ksend[0, 4:8, :] = jbuf[0, 31, 4:8, :]
            copy = pltpu.make_async_remote_copy(
                src_ref=ksend.at[it, rows], dst_ref=kbuf.at[it, rows],
                send_sem=k_send.at[it], recv_sem=k_recv.at[it],
                device_id=twin, device_id_type=MESH,
            )
            copy.start()
            sends.append(copy)
            if it == 0:
                ghost_step(0)
            total = weigh(0)
            if it == 0:
                tsend[...] = total
                ghost_step(1)
            copy.wait_recv()
            return total + kbuf[it, 0:4, :], sends

        def ghost_copy(part, side):
            target = (twin_tm if part == 0 else tm, slab - 1 if side == 0 else slab + 1)
            return pltpu.make_async_remote_copy(
                src_ref=ksend.at[0, pl.ds(0, 4)] if part == 0 else tsend,
                dst_ref=ghost.at[part, 1 - side],
                send_sem=g_send.at[part, side], recv_sem=g_recv.at[part, 1 - side],
                device_id=target, device_id_type=MESH,
            )

        def ghost_step(part):
            @pl.when(has_high)
            def _():
                ghost_copy(part, 1).start()

            @pl.when(has_low)
            def _():
                ghost_copy(part, 0).start()

        peers = sorted(
            [(dx, dy) for dx in range(4) for dy in range(8) if dx + dy > 0],
            key=lambda p: -min(p[0], 4 - p[0]) - min(p[1], 8 - p[1]),
        )
        pending = []
        fine()

        def detach():
            means = slab_means()
            for zc in range(4):
                for i in range(4):
                    k = HALO + 4 * zc + i
                    for half in range(2):
                        u[k, half] = u[k, half] - means[zc]
            return pack(means)

        end_mean = detach()
        jump = end_mean - decay * start_mean

        def halo2(side):
            peer = (tm, slab - 1) if side == 0 else (tm, slab + 1)
            rows = pl.ds(HALO, HALO) if side == 0 else pl.ds(LAYERS, HALO)
            return pltpu.make_async_remote_copy(
                src_ref=u.at[rows], dst_ref=dhalo.at[1 - side],
                send_sem=d_send.at[side], recv_sem=d_recv.at[side],
                device_id=peer, device_id_type=MESH,
            )

        def between1():
            @pl.when(has_high)
            def _():
                halo2(1).start()

            @pl.when(has_low)
            def _():
                halo2(0).start()

            powers(1)

            @pl.when(zz == 1)
            def _():
                pl.semaphore_wait(up, 1)

        pl.semaphore_wait(ring, 4)
        tell(cross, (plane_peer(0, 2), plane_peer(0, 6)))

        @pl.when(zz == 0)
        def _():
            pl.semaphore_wait(up, 1)
            tell(up, (twin,))

        pl.semaphore_wait(cross, 2)
        coarse, sends = coarse_solve(0, jump, between1)
        pending += sends

        @pl.when(has_high)
        def _():
            halo2(1).wait_send()

        @pl.when(has_low)
        def _():
            halo2(0).wait_send()

        for zc in range(4):
            wide = unpack(coarse[zc:zc + 1])
            for i in range(4):
                k = HALO + 4 * zc + i
                for half in range(2):
                    u[k, half] = u[k, half] + wide

        level2 = jnp.where(
            yy < 7, jbuf[0, 7, 4:5, :],
            jnp.where(xx < 3, jbuf[0, 31, 4:5, :], kbuf[0, 4:5, :]),
        )
        level2 = jnp.broadcast_to(level2, (8, 128))

        def reforce(k, _):
            for half in range(2):
                force[k, half] = level2 * src[k, half]
            return 0

        lax.fori_loop(0, EXT, reforce, 0, unroll=4)

        @pl.when(has_low)
        def _():
            halo2(1).wait_recv()
            for part in range(2):
                ghost_copy(part, 1).wait_recv()

        @pl.when(has_high)
        def _():
            halo2(0).wait_recv()
            for part in range(2):
                ghost_copy(part, 0).wait_recv()

        low_wide = {r: unpack(ghost[0, 0, r:r + 1, :] + ghost[1, 0, r:r + 1, :]) for r in (1, 2, 3)}
        high_wide = {r: unpack(ghost[0, 1, r:r + 1, :] + ghost[1, 1, r:r + 1, :]) for r in (0, 1, 2)}
        for i in range(HALO):
            for half in range(2):
                u[i, half] = dhalo[0, i, half] + low_wide[(LAYERS - HALO + i) // 4]
                u[HALO + LAYERS + i, half] = dhalo[1, i, half] + high_wide[i // 4]

        fine()

        end_mean = detach()
        jump = end_mean - decay * coarse
        final_copy = pltpu.make_async_remote_copy(
            src_ref=u.at[own], dst_ref=fin, send_sem=f_send, recv_sem=f_recv,
            device_id=(last, slab), device_id_type=MESH,
        )
        coarse, sends = coarse_solve(1, jump, final_copy.start)
        pending += sends
        wides = [unpack(coarse[zc:zc + 1]) for zc in range(4)]
        final_copy.wait_recv()
        for zc in range(4):
            for i in range(4):
                k = 4 * zc + i
                for half in range(2):
                    out[0, k, pl.ds(half, 8, stride=2), :] = fin[k, half] + wides[zc]

        for copy in pending:
            copy.wait_send()
        final_copy.wait_send()

        @pl.when(has_high)
        def _():
            for copy in halo_copies(1):
                copy.wait_send()
            for part in range(2):
                ghost_copy(part, 1).wait_send()

        @pl.when(has_low)
        def _():
            for copy in halo_copies(0):
                copy.wait_send()
            for part in range(2):
                ghost_copy(part, 0).wait_send()

    return kernel


def body(start_states, material, source, conductivity, tide_amp, phase, coarse_rate):
    f32 = jnp.float32
    smem = pl.BlockSpec(memory_space=pltpu.SMEM)
    hbm = pl.BlockSpec(memory_space=pl.ANY)
    vmem = pl.BlockSpec(memory_space=pltpu.VMEM)
    dma = pltpu.SemaphoreType.DMA
    regular = pltpu.SemaphoreType.REGULAR
    field = pltpu.VMEM((EXT, 2, 8, 128), f32)
    return pl.pallas_call(
        make_kernel(),
        out_shape=jax.ShapeDtypeStruct((1, LAYERS, 16, 128), f32),
        in_specs=[hbm, hbm, hbm, smem, smem, smem, vmem],
        out_specs=vmem,
        scratch_shapes=[
            pltpu.VMEM((EXT, 16, 128), f32),
            pltpu.VMEM((EXT, 16, 128), jnp.int32),
            pltpu.VMEM((EXT, 16, 128), f32),
            field, field, field, field,
            pltpu.VMEM((2, 32, 8, 128), f32),
            pltpu.VMEM((2, 8, 128), f32),
            pltpu.VMEM((2, 8, 128), f32),
            pltpu.VMEM((4, 128), f32),
            pltpu.VMEM((2, 2, 4, 128), f32),
            pltpu.VMEM((2, 2, 32, 4, 128), f32),
            pltpu.VMEM((2, HALO, 2, 8, 128), f32),
            pltpu.VMEM((LAYERS, 2, 8, 128), f32),
            dma((3,)), dma((2, 3)), dma((2, 3)),
            dma((2, 32)), dma((2, 32)), dma((2,)), dma((2,)),
            dma((2,)), dma((2,)), dma((2, 2)), dma((2, 2)),
            dma(()), dma(()), regular, regular, regular, regular,
        ],
        compiler_params=pltpu.CompilerParams(collective_id=0, has_side_effects=True),
    )(start_states, material, source, conductivity, tide_amp, phase, coarse_rate)


def solution(mesh):
    placed = (
        P("tm", "space", None, None),
        P("space", None, None),
        P("space", None, None),
        P(),
        P(),
        P("tm"),
        P("space", None, None),
    )
    return jax.shard_map(
        body, mesh=mesh, in_specs=placed, out_specs=P("tm", "space", None, None), check_vma=False
    )
```

```python
import jax
import jax.numpy as jnp
from jax import lax
from jax.experimental import pallas as pl
from jax.experimental.pallas import tpu as pltpu
from jax.sharding import PartitionSpec as P

FINE = 10
WINDOWS = 64
SLABS = 8
LAYERS = 16
HALO = FINE
EXT = LAYERS + 2 * HALO
MESH = pl.DeviceIdType.MESH


def roll(x, shift, axis):
    return pltpu.roll(x, shift % x.shape[axis], axis)


def make_kernel():
    def kernel(
        start, material, source, cond_in, amp_in, phase_in, rate_in, out,
        cond, amp, phase, rate, low_edge, high_edge,
        nat_u, nat_m, nat_s, u, coef, force, src, jbuf, ksend, kbuf, tsend,
        ghost, weight, dhalo, fin,
        loc_sem, h_send, h_recv, j_send, j_recv, k_send, k_recv,
        d_send, d_recv, g_send, g_recv, f_send, f_recv, near, ring, cross, up,
    ):
        tm = lax.axis_index("tm")
        slab = lax.axis_index("space")
        yy = lax.rem(tm, 8)
        group = tm // 8
        xx = lax.rem(group, 4)
        zz = group // 4
        has_low = slab > 0
        has_high = slab < SLABS - 1

        def plane_peer(dx, dy):
            x, y = lax.rem(xx + dx, 4), lax.rem(yy + dy, 8)
            return ((zz * 4 + x) * 8 + y, slab)

        twin_tm = lax.rem(tm + 32, WINDOWS)
        twin = (twin_tm, slab)
        last = lax.rem(tm + 2, WINDOWS)

        barrier = pltpu.get_barrier_semaphore()

        def greet(peer):
            pl.semaphore_signal(barrier, inc=1, device_id=peer, device_id_type=MESH)

        @pl.when(has_low)
        def _():
            greet((tm, slab - 1))

        @pl.when(has_high)
        def _():
            greet((tm, slab + 1))

        for dx, dy in ((0, 1), (0, 7), (1, 0), (3, 0)):
            greet(plane_peer(dx, dy))

        @pl.when(zz == 0)
        def _():
            greet(twin)

        own = pl.ds(HALO, LAYERS)
        small = [(phase_in, phase), (amp_in, amp), (cond_in, cond), (rate_in, rate)]
        small = [pltpu.make_async_copy(a, b, loc_sem.at[3 + i]) for i, (a, b) in enumerate(small)]
        locals_ = [
            pltpu.make_async_copy(start.at[0], nat_u.at[own], loc_sem.at[0]),
            pltpu.make_async_copy(material, nat_m.at[own], loc_sem.at[1]),
            pltpu.make_async_copy(source, nat_s.at[own], loc_sem.at[2]),
        ]
        for copy in small + locals_:
            copy.start()

        def tell(sem, peers):
            for peer in peers:
                pl.semaphore_signal(sem, inc=1, device_id=peer, device_id_type=MESH)

        sides = jnp.where(has_low, 1, 0) + jnp.where(has_high, 1, 0)
        pl.semaphore_wait(barrier, 4 + sides + zz)

        def halo_copies(side):
            peer = (tm, slab - 1) if side == 0 else (tm, slab + 1)
            rows = pl.ds(0, HALO) if side == 0 else pl.ds(LAYERS - HALO, HALO)
            ghost = pl.ds(HALO + LAYERS, HALO) if side == 0 else pl.ds(0, HALO)
            sources = (start.at[0, rows], material.at[rows], source.at[rows])
            targets = (nat_u.at[ghost], nat_m.at[ghost], nat_s.at[ghost])
            return [
                pltpu.make_async_remote_copy(
                    src_ref=a, dst_ref=b, send_sem=h_send.at[side, i],
                    recv_sem=h_recv.at[side, i], device_id=peer, device_id_type=MESH,
                )
                for i, (a, b) in enumerate(zip(sources, targets))
            ]

        @pl.when(has_high)
        def _():
            for copy in halo_copies(1):
                copy.start()

        @pl.when(has_low)
        def _():
            for copy in halo_copies(0):
                copy.start()

        @pl.when(zz == 1)
        def _():
            tell(up, (twin,))

        around = tuple(plane_peer(dx, dy) for dx, dy in ((0, 1), (0, 7), (1, 0), (3, 0)))
        tell(near, around)

        sub = lax.broadcasted_iota(jnp.int32, (8, 128), 0)
        lane = lax.broadcasted_iota(jnp.int32, (8, 128), 1)
        first_lane, last_lane = lane == 0, lane == 127
        first_sub, last_sub = sub == 0, sub == 7
        even_sub, even_lane = (sub & 1) == 0, (lane & 1) == 0
        low_pair = (lane & 3) < 2
        owner = (sub >> 1) == (lane & 3)
        pick = sub == 2 * (lane & 3)
        zero = jnp.zeros((8, 128), jnp.float32)

        def lane_total(x):
            x = x + jnp.where(even_lane, roll(x, -1, 1), roll(x, 1, 1))
            return x + jnp.where(low_pair, roll(x, -2, 1), roll(x, 2, 1))

        def block_mean(layers):
            total = layers[0]
            for part in layers[1:]:
                total = total + part
            total = total + jnp.where(even_sub, roll(total, -1, 0), roll(total, 1, 0))
            return lane_total(total) * (1.0 / 64.0)

        def pack(means):
            rows = [
                jnp.sum(jnp.where(pick, m, zero), axis=0, keepdims=True) for m in means
            ]
            return jnp.concatenate(rows, axis=0)

        def unpack(row):
            wide = jnp.broadcast_to(row, (8, 128))
            return lane_total(jnp.where(owner, wide, zero))

        def clear(side):
            def go(i, _):
                k = i + (HALO + LAYERS if side else 0)
                nat_u[k] = jnp.zeros((16, 128), jnp.float32)
                nat_s[k] = jnp.zeros((16, 128), jnp.float32)
                nat_m[k] = jnp.zeros((16, 128), jnp.int32)
                dhalo[side, i] = jnp.zeros((2, 8, 128), jnp.float32)
                return 0

            lax.fori_loop(0, HALO, go, 0)
            for part in range(2):
                ghost[part, side] = jnp.zeros((4, 128), jnp.float32)

        @pl.when(jnp.logical_not(has_low))
        def _():
            clear(0)

        @pl.when(jnp.logical_not(has_high))
        def _():
            clear(1)

        for copy in small:
            copy.wait()
        level_own = amp[phase[0]]
        jbuf[0, 0, 4:8, :] = jnp.full((4, 128), level_own, jnp.float32)

        spread_row = lax.broadcasted_iota(jnp.int32, (32, 128), 0)
        spread_col = lax.broadcasted_iota(jnp.int32, (32, 128), 1)
        spread = jnp.where(spread_row == (spread_col >> 2), 1.0, 0.0).astype(jnp.float32)
        quarter = lax.broadcasted_iota(jnp.int32, (4, 128), 0) == (
            lax.broadcasted_iota(jnp.int32, (4, 128), 1) & 3
        )
        rows = []
        for zc in range(4):
            wide = jnp.dot(
                rate[zc], spread, precision=lax.Precision.HIGHEST,
                preferred_element_type=jnp.float32,
            )
            rows.append(jnp.sum(jnp.where(quarter, wide, 0.0), axis=0, keepdims=True))
        packed_rate = jnp.concatenate(rows, axis=0)
        step_rate = packed_rate * (-1.0 / WINDOWS)
        decay = jnp.exp(step_rate)
        unclose = 1.0 / (1.0 - jnp.exp(-packed_rate))

        def powers(it):
            def go(i, _):
                dx, dy = i // 8, lax.rem(i, 8)
                lag = (xx - lax.rem(xx - dx + 4, 4)) * 8 + yy - lax.rem(yy - dy + 8, 8)
                for half in range(2):
                    power = lax.rem(lag - 2 * it + 32 * half + 2 * WINDOWS, WINDOWS)
                    weight[it, half, i] = jnp.exp(step_rate * power.astype(jnp.float32)) * unclose
                return 0

            lax.fori_loop(0, 32, go, 0, unroll=4)

        def lookup(m):
            picks = [cond[i] for i in range(16)]
            for bit in range(4):
                on = (m & (1 << bit)) != 0
                picks = [
                    jnp.where(on, picks[2 * i + 1], picks[2 * i])
                    for i in range(len(picks) // 2)
                ]
            return picks[0]

        level1 = level_own

        def arrange(lo, count, gain):
            def go(i, _):
                for half in range(2):
                    rows = pl.ds(half, 8, stride=2)
                    k = lo + i
                    u[k, half] = nat_u[k, rows, :]
                    c = lookup(nat_m[k, rows, :])
                    coef[k, half] = c if gain is None else c * gain
                    s = nat_s[k, rows, :]
                    src[k, half] = s
                    force[k, half] = level1 * s
                return 0

            lax.fori_loop(0, count, go, 0, unroll=2)

        for copy in locals_:
            copy.wait()
        pl.semaphore_wait(near, 4)
        tell(ring, tuple(plane_peer(dx, dy) for dx, dy in ((0, 2), (0, 6), (1, 0), (3, 0))))
        arrange(HALO, LAYERS, None)

        def slab_means():
            means = []
            for zc in range(4):
                base = HALO + 4 * zc
                means.append(
                    block_mean([u[base + i, half] for i in range(4) for half in range(2)])
                )
            return means

        start_mean = pack(slab_means())

        def advance(k, before, here, after):
            even, odd = here
            across = (
                odd + jnp.where(first_sub, zero, roll(odd, 1, 0)),
                even + jnp.where(last_sub, zero, roll(even, -1, 0)),
            )
            for half in range(2):
                now = here[half]
                total = before[half] + after[half] + across[half]
                total = total + jnp.where(first_lane, zero, roll(now, 1, 1))
                total = total + jnp.where(last_lane, zero, roll(now, -1, 1))
                u[k, half] = now + coef[k, half] * (total - 6.0 * now) + force[k, half]

        def layer(ref, k):
            return ref[k, 0], ref[k, 1]

        def sweep(base, lo, hi, below=None, above=None):
            before = below if below is not None else layer(u, base + lo - 1)
            here = layer(u, base + lo)
            for k in range(lo, hi):
                after = above if above is not None and k == hi - 1 else layer(u, base + k + 1)
                advance(base + k, before, here, after)
                before, here = here, after

        def inner():
            for t in range(1, 8):
                lo, hi = HALO + t, HALO + LAYERS - t
                for half in range(2):
                    low_edge[t, half] = u[lo, half]
                    high_edge[t, half] = u[hi - 1, half]
                sweep(0, lo, hi)

        def outer():
            for t in range(1, 8):
                sweep(0, t, HALO + t, above=layer(low_edge, t))
                sweep(0, EXT - HALO - t, EXT - t, below=layer(high_edge, t))

            def rest(i, _):
                sweep(0, 8, EXT - 8)
                return 0

            lax.fori_loop(0, 3, rest, 0)

        inner()
        pl.semaphore_wait(ring, 4)
        tell(cross, (plane_peer(0, 2), plane_peer(0, 6)))

        @pl.when(has_low)
        def _():
            for copy in halo_copies(1):
                copy.wait_recv()

        @pl.when(has_high)
        def _():
            for copy in halo_copies(0):
                copy.wait_recv()

        arrange(0, HALO, jnp.where(has_low, 1.0, 0.0))
        arrange(HALO + LAYERS, HALO, jnp.where(has_high, 1.0, 0.0))

        def pl_all(it, rows, sem):
            every = jbuf.at[it, pl.ds(1, 31), rows]
            return pltpu.make_async_copy(every, every, sem.at[it])

        def coarse_solve(it, jump, between):
            rows = pl.ds(0, 8 if it == 0 else 4)
            jbuf[it, 0, 0:4, :] = jump
            for dx, dy in peers:
                pltpu.make_async_remote_copy(
                    src_ref=jbuf.at[it, 0, rows], dst_ref=jbuf.at[it, 8 * dx + dy, rows],
                    send_sem=j_send.at[it], recv_sem=j_recv.at[it],
                    device_id=plane_peer(dx, dy), device_id_type=MESH,
                ).start()
            between()
            pl_all(it, rows, j_recv).wait()

            def weigh(half):
                terms = [weight[it, half, i] * jbuf[it, i, 0:4, :] for i in range(32)]
                while len(terms) > 1:
                    terms = [a + b for a, b in zip(terms[::2], terms[1::2])]
                return terms[0]

            ksend[it, 0:4, :] = weigh(1)
            if it == 0:
                ksend[0, 4:8, :] = jbuf[0, 31, 4:8, :]
            copy = pltpu.make_async_remote_copy(
                src_ref=ksend.at[it, rows], dst_ref=kbuf.at[it, rows],
                send_sem=k_send.at[it], recv_sem=k_recv.at[it],
                device_id=twin, device_id_type=MESH,
            )
            copy.start()
            if it == 0:
                ghost_step(0)
            total = weigh(0)
            if it == 0:
                tsend[...] = total
                ghost_step(1)
            copy.wait_recv()
            return total + kbuf[it, 0:4, :], [copy]

        def ghost_copy(part, side):
            target = (twin_tm if part == 0 else tm, slab - 1 if side == 0 else slab + 1)
            return pltpu.make_async_remote_copy(
                src_ref=ksend.at[0, pl.ds(0, 4)] if part == 0 else tsend,
                dst_ref=ghost.at[part, 1 - side],
                send_sem=g_send.at[part, side], recv_sem=g_recv.at[part, 1 - side],
                device_id=target, device_id_type=MESH,
            )

        def ghost_step(part):
            @pl.when(has_high)
            def _():
                ghost_copy(part, 1).start()

            @pl.when(has_low)
            def _():
                ghost_copy(part, 0).start()

        peers = sorted(
            [(dx, dy) for dx in range(4) for dy in range(8) if dx + dy > 0],
            key=lambda p: -min(p[0], 4 - p[0]) - min(p[1], 8 - p[1]),
        )
        pending = []
        outer()

        def detach():
            means = slab_means()
            for zc in range(4):
                for i in range(4):
                    k = HALO + 4 * zc + i
                    for half in range(2):
                        u[k, half] = u[k, half] - means[zc]
            return pack(means)

        end_mean = detach()
        jump = end_mean - decay * start_mean

        def halo2(side):
            peer = (tm, slab - 1) if side == 0 else (tm, slab + 1)
            rows = pl.ds(HALO, HALO) if side == 0 else pl.ds(LAYERS, HALO)
            return pltpu.make_async_remote_copy(
                src_ref=u.at[rows], dst_ref=dhalo.at[1 - side],
                send_sem=d_send.at[side], recv_sem=d_recv.at[side],
                device_id=peer, device_id_type=MESH,
            )

        def between1():
            @pl.when(has_high)
            def _():
                halo2(1).start()

            @pl.when(has_low)
            def _():
                halo2(0).start()

            powers(0)
            powers(1)

            @pl.when(zz == 0)
            def _():
                pl.semaphore_wait(up, 1)
                tell(up, (twin,))

            @pl.when(zz == 1)
            def _():
                pl.semaphore_wait(up, 1)

        pl.semaphore_wait(cross, 2)
        coarse, sends = coarse_solve(0, jump, between1)
        pending += sends

        @pl.when(has_high)
        def _():
            halo2(1).wait_send()

        @pl.when(has_low)
        def _():
            halo2(0).wait_send()

        for zc in range(4):
            wide = unpack(coarse[zc:zc + 1])
            for i in range(4):
                k = HALO + 4 * zc + i
                for half in range(2):
                    u[k, half] = u[k, half] + wide

        level2 = jnp.where(
            yy < 7, jbuf[0, 7, 4:5, :],
            jnp.where(xx < 3, jbuf[0, 31, 4:5, :], kbuf[0, 4:5, :]),
        )
        level2 = jnp.broadcast_to(level2, (8, 128))

        def reforce(k, _):
            for half in range(2):
                force[k, half] = level2 * src[k, half]
            return 0

        lax.fori_loop(0, EXT, reforce, 0, unroll=4)
        inner()

        @pl.when(has_low)
        def _():
            halo2(1).wait_recv()
            for part in range(2):
                ghost_copy(part, 1).wait_recv()

        @pl.when(has_high)
        def _():
            halo2(0).wait_recv()
            for part in range(2):
                ghost_copy(part, 0).wait_recv()

        low_wide = {r: unpack(ghost[0, 0, r:r + 1, :] + ghost[1, 0, r:r + 1, :]) for r in (1, 2, 3)}
        high_wide = {r: unpack(ghost[0, 1, r:r + 1, :] + ghost[1, 1, r:r + 1, :]) for r in (0, 1, 2)}
        for i in range(HALO):
            for half in range(2):
                u[i, half] = dhalo[0, i, half] + low_wide[(LAYERS - HALO + i) // 4]
                u[HALO + LAYERS + i, half] = dhalo[1, i, half] + high_wide[i // 4]

        outer()

        end_mean = detach()
        jump = end_mean - decay * coarse
        final_copy = pltpu.make_async_remote_copy(
            src_ref=u.at[own], dst_ref=fin, send_sem=f_send, recv_sem=f_recv,
            device_id=(last, slab), device_id_type=MESH,
        )
        coarse, sends = coarse_solve(1, jump, final_copy.start)
        pending += sends
        wides = [unpack(coarse[zc:zc + 1]) for zc in range(4)]
        final_copy.wait_recv()
        for zc in range(4):
            for i in range(4):
                k = 4 * zc + i
                for half in range(2):
                    out[0, k, pl.ds(half, 8, stride=2), :] = fin[k, half] + wides[zc]

        for copy in pending:
            copy.wait_send()
        pl_all(0, pl.ds(0, 8), j_send).wait()
        pl_all(1, pl.ds(0, 4), j_send).wait()
        final_copy.wait_send()

        @pl.when(has_high)
        def _():
            for copy in halo_copies(1):
                copy.wait_send()
            for part in range(2):
                ghost_copy(part, 1).wait_send()

        @pl.when(has_low)
        def _():
            for copy in halo_copies(0):
                copy.wait_send()
            for part in range(2):
                ghost_copy(part, 0).wait_send()

    return kernel


def body(start_states, material, source, conductivity, tide_amp, phase, coarse_rate):
    f32 = jnp.float32
    hbm = pl.BlockSpec(memory_space=pl.ANY)
    vmem = pl.BlockSpec(memory_space=pltpu.VMEM)
    dma = pltpu.SemaphoreType.DMA
    regular = pltpu.SemaphoreType.REGULAR
    field = pltpu.VMEM((EXT, 2, 8, 128), f32)
    return pl.pallas_call(
        make_kernel(),
        out_shape=jax.ShapeDtypeStruct((1, LAYERS, 16, 128), f32),
        in_specs=[hbm] * 7,
        out_specs=vmem,
        scratch_shapes=[
            pltpu.SMEM((16,), f32),
            pltpu.SMEM((12,), f32),
            pltpu.SMEM((1,), jnp.int32),
            pltpu.VMEM((4, 4, 32), f32),
            pltpu.VMEM((8, 2, 8, 128), f32),
            pltpu.VMEM((8, 2, 8, 128), f32),
            pltpu.VMEM((EXT, 16, 128), f32),
            pltpu.VMEM((EXT, 16, 128), jnp.int32),
            pltpu.VMEM((EXT, 16, 128), f32),
            field, field, field, field,
            pltpu.VMEM((2, 32, 8, 128), f32),
            pltpu.VMEM((2, 8, 128), f32),
            pltpu.VMEM((2, 8, 128), f32),
            pltpu.VMEM((4, 128), f32),
            pltpu.VMEM((2, 2, 4, 128), f32),
            pltpu.VMEM((2, 2, 32, 4, 128), f32),
            pltpu.VMEM((2, HALO, 2, 8, 128), f32),
            pltpu.VMEM((LAYERS, 2, 8, 128), f32),
            dma((7,)), dma((2, 3)), dma((2, 3)),
            dma((2,)), dma((2,)), dma((2,)), dma((2,)),
            dma((2,)), dma((2,)), dma((2, 2)), dma((2, 2)),
            dma(()), dma(()), regular, regular, regular, regular,
        ],
        compiler_params=pltpu.CompilerParams(collective_id=0, has_side_effects=True),
    )(start_states, material, source, conductivity, tide_amp, phase, coarse_rate)


def solution(mesh):
    placed = (
        P("tm", "space", None, None),
        P("space", None, None),
        P("space", None, None),
        P(),
        P(),
        P("tm"),
        P("space", None, None),
    )
    return jax.shard_map(
        body, mesh=mesh, in_specs=placed, out_specs=P("tm", "space", None, None), check_vma=False
    )
```

```python
import jax
import jax.numpy as jnp
from jax import lax
from jax.experimental import pallas as pl
from jax.experimental.pallas import tpu as pltpu
from jax.sharding import PartitionSpec as P

FINE = 10
WINDOWS = 64
SLABS = 8
LAYERS = 16
HALO = FINE
VMEM_BYTES = 16 * 2**20
EXT = LAYERS + 2 * HALO
MESH = pl.DeviceIdType.MESH


def roll(x, shift, axis):
    return pltpu.roll(x, shift % x.shape[axis], axis)


def make_kernel():
    def kernel(
        start, material, source, cond_in, amp_in, phase_in, rate_in, out,
        cond, amp, phase, rate, result, low_edge, high_edge,
        nat_u, nat_m, nat_s, u, coef, force, src, jbuf, ksend, kbuf, tsend,
        ghost, weight, dhalo, fin,
        loc_sem, h_send, h_recv, j_send, j_recv, k_send, k_recv,
        d_send, d_recv, g_send, g_recv, f_send, f_recv, f_out, near, ring, cross, up,
    ):
        tm = lax.axis_index("tm")
        slab = lax.axis_index("space")
        yy = lax.rem(tm, 8)
        group = tm // 8
        xx = lax.rem(group, 4)
        zz = group // 4
        has_low = slab > 0
        has_high = slab < SLABS - 1

        def plane_peer(dx, dy):
            x, y = lax.rem(xx + dx, 4), lax.rem(yy + dy, 8)
            return ((zz * 4 + x) * 8 + y, slab)

        twin_tm = lax.rem(tm + 32, WINDOWS)
        twin = (twin_tm, slab)
        last = lax.rem(tm + 2, WINDOWS)

        barrier = pltpu.get_barrier_semaphore()

        def greet(peer):
            pl.semaphore_signal(barrier, inc=1, device_id=peer, device_id_type=MESH)

        @pl.when(has_low)
        def _():
            greet((tm, slab - 1))

        @pl.when(has_high)
        def _():
            greet((tm, slab + 1))

        for dx, dy in ((0, 1), (0, 7), (1, 0), (3, 0)):
            greet(plane_peer(dx, dy))

        @pl.when(zz == 0)
        def _():
            greet(twin)

        own = pl.ds(HALO, LAYERS)
        small = [(phase_in, phase), (amp_in, amp), (cond_in, cond), (rate_in, rate)]
        small = [pltpu.make_async_copy(a, b, loc_sem.at[3 + i]) for i, (a, b) in enumerate(small)]
        locals_ = [
            pltpu.make_async_copy(start.at[0], nat_u.at[own], loc_sem.at[0]),
            pltpu.make_async_copy(material, nat_m.at[own], loc_sem.at[1]),
            pltpu.make_async_copy(source, nat_s.at[own], loc_sem.at[2]),
        ]
        for copy in small + locals_:
            copy.start()

        def tell(sem, peers):
            for peer in peers:
                pl.semaphore_signal(sem, inc=1, device_id=peer, device_id_type=MESH)

        sides = jnp.where(has_low, 1, 0) + jnp.where(has_high, 1, 0)
        pl.semaphore_wait(barrier, 4 + sides + zz)

        def halo_copies(side):
            peer = (tm, slab - 1) if side == 0 else (tm, slab + 1)
            rows = pl.ds(0, HALO) if side == 0 else pl.ds(LAYERS - HALO, HALO)
            ghost = pl.ds(HALO + LAYERS, HALO) if side == 0 else pl.ds(0, HALO)
            sources = (start.at[0, rows], material.at[rows], source.at[rows])
            targets = (nat_u.at[ghost], nat_m.at[ghost], nat_s.at[ghost])
            return [
                pltpu.make_async_remote_copy(
                    src_ref=a, dst_ref=b, send_sem=h_send.at[side, i],
                    recv_sem=h_recv.at[side, i], device_id=peer, device_id_type=MESH,
                )
                for i, (a, b) in enumerate(zip(sources, targets))
            ]

        @pl.when(has_high)
        def _():
            for copy in halo_copies(1):
                copy.start()

        @pl.when(has_low)
        def _():
            for copy in halo_copies(0):
                copy.start()

        @pl.when(zz == 1)
        def _():
            tell(up, (twin,))

        around = tuple(plane_peer(dx, dy) for dx, dy in ((0, 1), (0, 7), (1, 0), (3, 0)))
        tell(near, around)

        sub = lax.broadcasted_iota(jnp.int32, (8, 128), 0)
        lane = lax.broadcasted_iota(jnp.int32, (8, 128), 1)
        first_lane, last_lane = lane == 0, lane == 127
        first_sub, last_sub = sub == 0, sub == 7
        even_sub, even_lane = (sub & 1) == 0, (lane & 1) == 0
        low_pair = (lane & 3) < 2
        owner = (sub >> 1) == (lane & 3)
        pick = sub == 2 * (lane & 3)
        zero = jnp.zeros((8, 128), jnp.float32)

        def lane_total(x):
            x = x + jnp.where(even_lane, roll(x, -1, 1), roll(x, 1, 1))
            return x + jnp.where(low_pair, roll(x, -2, 1), roll(x, 2, 1))

        def block_mean(layers):
            total = layers[0]
            for part in layers[1:]:
                total = total + part
            total = total + jnp.where(even_sub, roll(total, -1, 0), roll(total, 1, 0))
            return lane_total(total) * (1.0 / 64.0)

        def pack(means):
            rows = [
                jnp.sum(jnp.where(pick, m, zero), axis=0, keepdims=True) for m in means
            ]
            return jnp.concatenate(rows, axis=0)

        def unpack(row):
            wide = jnp.broadcast_to(row, (8, 128))
            return lane_total(jnp.where(owner, wide, zero))

        def clear(side):
            def go(i, _):
                k = i + (HALO + LAYERS if side else 0)
                nat_u[k] = jnp.zeros((16, 128), jnp.float32)
                nat_s[k] = jnp.zeros((16, 128), jnp.float32)
                nat_m[k] = jnp.zeros((16, 128), jnp.int32)
                dhalo[side, i] = jnp.zeros((2, 8, 128), jnp.float32)
                return 0

            lax.fori_loop(0, HALO, go, 0)
            for part in range(2):
                ghost[part, side] = jnp.zeros((4, 128), jnp.float32)

        @pl.when(jnp.logical_not(has_low))
        def _():
            clear(0)

        @pl.when(jnp.logical_not(has_high))
        def _():
            clear(1)

        for copy in small:
            copy.wait()
        level_own = amp[phase[0]]
        jbuf[0, 0, 4:8, :] = jnp.full((4, 128), level_own, jnp.float32)

        spread_row = lax.broadcasted_iota(jnp.int32, (32, 128), 0)
        spread_col = lax.broadcasted_iota(jnp.int32, (32, 128), 1)
        spread = jnp.where(spread_row == (spread_col >> 2), 1.0, 0.0).astype(jnp.float32)
        quarter = lax.broadcasted_iota(jnp.int32, (4, 128), 0) == (
            lax.broadcasted_iota(jnp.int32, (4, 128), 1) & 3
        )
        rows = []
        for zc in range(4):
            wide = jnp.dot(
                rate[zc], spread, precision=lax.Precision.HIGHEST,
                preferred_element_type=jnp.float32,
            )
            rows.append(jnp.sum(jnp.where(quarter, wide, 0.0), axis=0, keepdims=True))
        packed_rate = jnp.concatenate(rows, axis=0)
        step_rate = packed_rate * (-1.0 / WINDOWS)
        decay = jnp.exp(step_rate)
        unclose = 1.0 / (1.0 - jnp.exp(-packed_rate))

        def powers(it):
            def go(i, _):
                dx, dy = i // 8, lax.rem(i, 8)
                lag = (xx - lax.rem(xx - dx + 4, 4)) * 8 + yy - lax.rem(yy - dy + 8, 8)
                for half in range(2):
                    power = lax.rem(lag - 2 * it + 32 * half + 2 * WINDOWS, WINDOWS)
                    weight[it, half, i] = jnp.exp(step_rate * power.astype(jnp.float32)) * unclose
                return 0

            lax.fori_loop(0, 32, go, 0, unroll=4)

        def lookup(m):
            picks = [cond[i] for i in range(16)]
            for bit in range(4):
                on = (m & (1 << bit)) != 0
                picks = [
                    jnp.where(on, picks[2 * i + 1], picks[2 * i])
                    for i in range(len(picks) // 2)
                ]
            return picks[0]

        level1 = level_own

        def arrange(lo, count, gain):
            def go(i, _):
                for half in range(2):
                    rows = pl.ds(half, 8, stride=2)
                    k = lo + i
                    u[k, half] = nat_u[k, rows, :]
                    c = lookup(nat_m[k, rows, :])
                    coef[k, half] = c if gain is None else c * gain
                    s = nat_s[k, rows, :]
                    src[k, half] = s
                    force[k, half] = level1 * s
                return 0

            lax.fori_loop(0, count, go, 0, unroll=2)

        for copy in locals_:
            copy.wait()
        pl.semaphore_wait(near, 4)
        tell(ring, tuple(plane_peer(dx, dy) for dx, dy in ((0, 2), (0, 6), (1, 0), (3, 0))))
        arrange(HALO, LAYERS, None)

        def slab_means():
            means = []
            for zc in range(4):
                base = HALO + 4 * zc
                means.append(
                    block_mean([u[base + i, half] for i in range(4) for half in range(2)])
                )
            return means

        start_mean = pack(slab_means())

        def advance(k, before, here, after):
            even, odd = here
            across = (
                odd + jnp.where(first_sub, zero, roll(odd, 1, 0)),
                even + jnp.where(last_sub, zero, roll(even, -1, 0)),
            )
            for half in range(2):
                now = here[half]
                total = before[half] + after[half] + across[half]
                total = total + jnp.where(first_lane, zero, roll(now, 1, 1))
                total = total + jnp.where(last_lane, zero, roll(now, -1, 1))
                u[k, half] = now + coef[k, half] * (total - 6.0 * now) + force[k, half]

        def layer(ref, k):
            return ref[k, 0], ref[k, 1]

        def sweep(base, lo, hi, below=None, above=None):
            before = below if below is not None else layer(u, base + lo - 1)
            here = layer(u, base + lo)
            for k in range(lo, hi):
                after = above if above is not None and k == hi - 1 else layer(u, base + k + 1)
                advance(base + k, before, here, after)
                before, here = here, after

        def inner():
            for t in range(1, 8):
                lo, hi = HALO + t, HALO + LAYERS - t
                for half in range(2):
                    low_edge[t, half] = u[lo, half]
                    high_edge[t, half] = u[hi - 1, half]
                sweep(0, lo, hi)

        def outer():
            for t in range(1, 8):
                sweep(0, t, HALO + t, above=layer(low_edge, t))
                sweep(0, EXT - HALO - t, EXT - t, below=layer(high_edge, t))

            def rest(i, _):
                sweep(0, 8, EXT - 8)
                return 0

            lax.fori_loop(0, 3, rest, 0)

        inner()
        pl.semaphore_wait(ring, 4)
        tell(cross, (plane_peer(0, 2), plane_peer(0, 6)))

        @pl.when(has_low)
        def _():
            for copy in halo_copies(1):
                copy.wait_recv()

        @pl.when(has_high)
        def _():
            for copy in halo_copies(0):
                copy.wait_recv()

        arrange(0, HALO, jnp.where(has_low, 1.0, 0.0))
        arrange(HALO + LAYERS, HALO, jnp.where(has_high, 1.0, 0.0))

        def pl_all(it, rows, sem):
            every = jbuf.at[it, pl.ds(1, 31), rows]
            return pltpu.make_async_copy(every, every, sem.at[it])

        def coarse_solve(it, jump, between):
            rows = pl.ds(0, 8 if it == 0 else 4)
            jbuf[it, 0, 0:4, :] = jump
            for dx, dy in peers:
                pltpu.make_async_remote_copy(
                    src_ref=jbuf.at[it, 0, rows], dst_ref=jbuf.at[it, 8 * dx + dy, rows],
                    send_sem=j_send.at[it], recv_sem=j_recv.at[it],
                    device_id=plane_peer(dx, dy), device_id_type=MESH,
                ).start()
            between()
            pl_all(it, rows, j_recv).wait()

            def weigh(half):
                terms = [weight[it, half, i] * jbuf[it, i, 0:4, :] for i in range(32)]
                while len(terms) > 1:
                    terms = [a + b for a, b in zip(terms[::2], terms[1::2])]
                return terms[0]

            ksend[it, 0:4, :] = weigh(1)
            if it == 0:
                ksend[0, 4:8, :] = jbuf[0, 31, 4:8, :]
            copy = pltpu.make_async_remote_copy(
                src_ref=ksend.at[it, rows], dst_ref=kbuf.at[it, rows],
                send_sem=k_send.at[it], recv_sem=k_recv.at[it],
                device_id=twin, device_id_type=MESH,
            )
            copy.start()
            if it == 0:
                ghost_step(0)
            total = weigh(0)
            if it == 0:
                tsend[...] = total
                ghost_step(1)
            copy.wait_recv()
            return total + kbuf[it, 0:4, :], [copy]

        def ghost_copy(part, side):
            target = (twin_tm if part == 0 else tm, slab - 1 if side == 0 else slab + 1)
            return pltpu.make_async_remote_copy(
                src_ref=ksend.at[0, pl.ds(0, 4)] if part == 0 else tsend,
                dst_ref=ghost.at[part, 1 - side],
                send_sem=g_send.at[part, side], recv_sem=g_recv.at[part, 1 - side],
                device_id=target, device_id_type=MESH,
            )

        def ghost_step(part):
            @pl.when(has_high)
            def _():
                ghost_copy(part, 1).start()

            @pl.when(has_low)
            def _():
                ghost_copy(part, 0).start()

        peers = sorted(
            [(dx, dy) for dx in range(4) for dy in range(8) if dx + dy > 0],
            key=lambda p: -min(p[0], 4 - p[0]) - min(p[1], 8 - p[1]),
        )
        pending = []
        outer()

        def detach():
            means = slab_means()
            for zc in range(4):
                for i in range(4):
                    k = HALO + 4 * zc + i
                    for half in range(2):
                        u[k, half] = u[k, half] - means[zc]
            return pack(means)

        end_mean = detach()
        jump = end_mean - decay * start_mean

        def halo2(side):
            peer = (tm, slab - 1) if side == 0 else (tm, slab + 1)
            rows = pl.ds(HALO, HALO) if side == 0 else pl.ds(LAYERS, HALO)
            return pltpu.make_async_remote_copy(
                src_ref=u.at[rows], dst_ref=dhalo.at[1 - side],
                send_sem=d_send.at[side], recv_sem=d_recv.at[side],
                device_id=peer, device_id_type=MESH,
            )

        def between1():
            @pl.when(has_high)
            def _():
                halo2(1).start()

            @pl.when(has_low)
            def _():
                halo2(0).start()

            powers(0)
            powers(1)

            @pl.when(zz == 0)
            def _():
                pl.semaphore_wait(up, 1)
                tell(up, (twin,))

            @pl.when(zz == 1)
            def _():
                pl.semaphore_wait(up, 1)

        pl.semaphore_wait(cross, 2)
        coarse, sends = coarse_solve(0, jump, between1)
        pending += sends

        @pl.when(has_high)
        def _():
            halo2(1).wait_send()

        @pl.when(has_low)
        def _():
            halo2(0).wait_send()

        for zc in range(4):
            wide = unpack(coarse[zc:zc + 1])
            for i in range(4):
                k = HALO + 4 * zc + i
                for half in range(2):
                    u[k, half] = u[k, half] + wide

        level2 = jnp.where(
            yy < 7, jbuf[0, 7, 4:5, :],
            jnp.where(xx < 3, jbuf[0, 31, 4:5, :], kbuf[0, 4:5, :]),
        )
        level2 = jnp.broadcast_to(level2, (8, 128))

        def reforce(k, _):
            for half in range(2):
                force[k, half] = level2 * src[k, half]
            return 0

        lax.fori_loop(0, EXT, reforce, 0, unroll=4)
        inner()

        @pl.when(has_low)
        def _():
            halo2(1).wait_recv()
            for part in range(2):
                ghost_copy(part, 1).wait_recv()

        @pl.when(has_high)
        def _():
            halo2(0).wait_recv()
            for part in range(2):
                ghost_copy(part, 0).wait_recv()

        low_wide = {r: unpack(ghost[0, 0, r:r + 1, :] + ghost[1, 0, r:r + 1, :]) for r in (1, 2, 3)}
        high_wide = {r: unpack(ghost[0, 1, r:r + 1, :] + ghost[1, 1, r:r + 1, :]) for r in (0, 1, 2)}
        for i in range(HALO):
            for half in range(2):
                u[i, half] = dhalo[0, i, half] + low_wide[(LAYERS - HALO + i) // 4]
                u[HALO + LAYERS + i, half] = dhalo[1, i, half] + high_wide[i // 4]

        outer()

        end_mean = detach()
        jump = end_mean - decay * coarse
        final_copy = pltpu.make_async_remote_copy(
            src_ref=u.at[own], dst_ref=fin, send_sem=f_send, recv_sem=f_recv,
            device_id=(last, slab), device_id_type=MESH,
        )
        coarse, sends = coarse_solve(1, jump, final_copy.start)
        pending += sends
        wides = [unpack(coarse[zc:zc + 1]) for zc in range(4)]
        final_copy.wait_recv()
        for zc in range(4):
            for i in range(4):
                k = 4 * zc + i
                for half in range(2):
                    result[k, pl.ds(half, 8, stride=2), :] = fin[k, half] + wides[zc]

        result_copy = pltpu.make_async_copy(result, out.at[0], f_out)
        result_copy.start()

        for copy in pending:
            copy.wait_send()
        pl_all(0, pl.ds(0, 8), j_send).wait()
        pl_all(1, pl.ds(0, 4), j_send).wait()
        final_copy.wait_send()
        result_copy.wait()

        @pl.when(has_high)
        def _():
            for copy in halo_copies(1):
                copy.wait_send()
            for part in range(2):
                ghost_copy(part, 1).wait_send()

        @pl.when(has_low)
        def _():
            for copy in halo_copies(0):
                copy.wait_send()
            for part in range(2):
                ghost_copy(part, 0).wait_send()

    return kernel


def body(start_states, material, source, conductivity, tide_amp, phase, coarse_rate):
    f32 = jnp.float32
    hbm = pl.BlockSpec(memory_space=pltpu.HBM)
    somewhere = pl.BlockSpec(memory_space=pl.ANY)
    dma = pltpu.SemaphoreType.DMA
    regular = pltpu.SemaphoreType.REGULAR
    field = pltpu.VMEM((EXT, 2, 8, 128), f32)
    return pl.pallas_call(
        make_kernel(),
        out_shape=jax.ShapeDtypeStruct((1, LAYERS, 16, 128), f32),
        in_specs=[hbm] * 7,
        out_specs=somewhere,
        scratch_shapes=[
            pltpu.SMEM((16,), f32),
            pltpu.SMEM((12,), f32),
            pltpu.SMEM((1,), jnp.int32),
            pltpu.VMEM((4, 4, 32), f32),
            pltpu.VMEM((LAYERS, 16, 128), f32),
            pltpu.VMEM((8, 2, 8, 128), f32),
            pltpu.VMEM((8, 2, 8, 128), f32),
            pltpu.VMEM((EXT, 16, 128), f32),
            pltpu.VMEM((EXT, 16, 128), jnp.int32),
            pltpu.VMEM((EXT, 16, 128), f32),
            field, field, field, field,
            pltpu.VMEM((2, 32, 8, 128), f32),
            pltpu.VMEM((2, 8, 128), f32),
            pltpu.VMEM((2, 8, 128), f32),
            pltpu.VMEM((4, 128), f32),
            pltpu.VMEM((2, 2, 4, 128), f32),
            pltpu.VMEM((2, 2, 32, 4, 128), f32),
            pltpu.VMEM((2, HALO, 2, 8, 128), f32),
            pltpu.VMEM((LAYERS, 2, 8, 128), f32),
            dma((7,)), dma((2, 3)), dma((2, 3)),
            dma((2,)), dma((2,)), dma((2,)), dma((2,)),
            dma((2,)), dma((2,)), dma((2, 2)), dma((2, 2)),
            dma(()), dma(()), dma(()), regular, regular, regular, regular,
        ],
        compiler_params=pltpu.CompilerParams(
            collective_id=0, has_side_effects=True, vmem_limit_bytes=VMEM_BYTES
        ),
    )(
        *(
            pltpu.with_memory_space_constraint(x, pltpu.HBM)
            for x in (start_states, material, source, conductivity, tide_amp)
        ),
        phase,
        pltpu.with_memory_space_constraint(coarse_rate, pltpu.HBM),
    )


def solution(mesh):
    placed = (
        P("tm", "space", None, None),
        P("space", None, None),
        P("space", None, None),
        P(),
        P(),
        P("tm"),
        P("space", None, None),
    )
    return jax.shard_map(
        body, mesh=mesh, in_specs=placed, out_specs=P("tm", "space", None, None), check_vma=False
    )
```

```python
import jax
import jax.numpy as jnp
from jax import lax
from jax.experimental import pallas as pl
from jax.experimental.pallas import tpu as pltpu
from jax.sharding import PartitionSpec as P

FINE = 10
WINDOWS = 64
SLABS = 8
LAYERS = 16
HALO = FINE
VMEM_BYTES = 16 * 2**20
EXT = LAYERS + 2 * HALO
MESH = pl.DeviceIdType.MESH


def roll(x, shift, axis):
    return pltpu.roll(x, shift % x.shape[axis], axis)


def make_kernel():
    def kernel(
        start, material, source, cond_in, amp_in, phase_in, rate_in, out,
        cond, amp, phase, rate, result, low_edge, high_edge,
        nat_u, nat_m, nat_s, u, coef, force, src, jbuf, ksend, kbuf, tsend,
        ghost, weight, dhalo, fin,
        loc_sem, h_send, h_recv, j_send, j_recv, k_send, k_recv,
        d_send, d_recv, g_send, g_recv, f_send, f_recv, f_out, near, ring, cross, up,
    ):
        tm = lax.axis_index("tm")
        slab = lax.axis_index("space")
        yy = lax.rem(tm, 8)
        group = tm // 8
        xx = lax.rem(group, 4)
        zz = group // 4
        has_low = slab > 0
        has_high = slab < SLABS - 1

        def plane_peer(dx, dy):
            x, y = lax.rem(xx + dx, 4), lax.rem(yy + dy, 8)
            return ((zz * 4 + x) * 8 + y, slab)

        twin_tm = lax.rem(tm + 32, WINDOWS)
        twin = (twin_tm, slab)
        last = lax.rem(tm + 2, WINDOWS)

        barrier = pltpu.get_barrier_semaphore()

        def greet(peer):
            pl.semaphore_signal(barrier, inc=1, device_id=peer, device_id_type=MESH)

        @pl.when(has_low)
        def _():
            greet((tm, slab - 1))

        @pl.when(has_high)
        def _():
            greet((tm, slab + 1))

        for dx, dy in ((0, 1), (0, 7), (1, 0), (3, 0)):
            greet(plane_peer(dx, dy))

        @pl.when(zz == 0)
        def _():
            greet(twin)

        own = pl.ds(HALO, LAYERS)
        small = [(phase_in, phase), (amp_in, amp), (cond_in, cond), (rate_in, rate)]
        small = [pltpu.make_async_copy(a, b, loc_sem.at[3 + i]) for i, (a, b) in enumerate(small)]
        locals_ = [
            pltpu.make_async_copy(start.at[0], nat_u.at[own], loc_sem.at[0]),
            pltpu.make_async_copy(material, nat_m.at[own], loc_sem.at[1]),
            pltpu.make_async_copy(source, nat_s.at[own], loc_sem.at[2]),
        ]
        for copy in small + locals_:
            copy.start()

        def tell(sem, peers):
            for peer in peers:
                pl.semaphore_signal(sem, inc=1, device_id=peer, device_id_type=MESH)

        sides = jnp.where(has_low, 1, 0) + jnp.where(has_high, 1, 0)
        pl.semaphore_wait(barrier, 4 + sides + zz)

        def halo_copies(side):
            peer = (tm, slab - 1) if side == 0 else (tm, slab + 1)
            rows = pl.ds(0, HALO) if side == 0 else pl.ds(LAYERS - HALO, HALO)
            ghost = pl.ds(HALO + LAYERS, HALO) if side == 0 else pl.ds(0, HALO)
            sources = (start.at[0, rows], material.at[rows], source.at[rows])
            targets = (nat_u.at[ghost], nat_m.at[ghost], nat_s.at[ghost])
            return [
                pltpu.make_async_remote_copy(
                    src_ref=a, dst_ref=b, send_sem=h_send.at[side, i],
                    recv_sem=h_recv.at[side, i], device_id=peer, device_id_type=MESH,
                )
                for i, (a, b) in enumerate(zip(sources, targets))
            ]

        @pl.when(has_high)
        def _():
            for copy in halo_copies(1):
                copy.start()

        @pl.when(has_low)
        def _():
            for copy in halo_copies(0):
                copy.start()

        @pl.when(zz == 1)
        def _():
            tell(up, (twin,))

        around = tuple(plane_peer(dx, dy) for dx, dy in ((0, 1), (0, 7), (1, 0), (3, 0)))
        tell(near, around)

        sub = lax.broadcasted_iota(jnp.int32, (8, 128), 0)
        lane = lax.broadcasted_iota(jnp.int32, (8, 128), 1)
        first_lane, last_lane = lane == 0, lane == 127
        first_sub, last_sub = sub == 0, sub == 7
        even_sub, even_lane = (sub & 1) == 0, (lane & 1) == 0
        low_pair = (lane & 3) < 2
        owner = (sub >> 1) == (lane & 3)
        pick = sub == 2 * (lane & 3)
        zero = jnp.zeros((8, 128), jnp.float32)

        def lane_total(x):
            x = x + jnp.where(even_lane, roll(x, -1, 1), roll(x, 1, 1))
            return x + jnp.where(low_pair, roll(x, -2, 1), roll(x, 2, 1))

        def block_mean(layers):
            total = layers[0]
            for part in layers[1:]:
                total = total + part
            total = total + jnp.where(even_sub, roll(total, -1, 0), roll(total, 1, 0))
            return lane_total(total) * (1.0 / 64.0)

        def pack(means):
            rows = [
                jnp.sum(jnp.where(pick, m, zero), axis=0, keepdims=True) for m in means
            ]
            return jnp.concatenate(rows, axis=0)

        def unpack(row):
            wide = jnp.broadcast_to(row, (8, 128))
            return lane_total(jnp.where(owner, wide, zero))

        def clear(side):
            def go(i, _):
                k = i + (HALO + LAYERS if side else 0)
                nat_u[k] = jnp.zeros((16, 128), jnp.float32)
                nat_s[k] = jnp.zeros((16, 128), jnp.float32)
                nat_m[k] = jnp.zeros((16, 128), jnp.int32)
                dhalo[side, i] = jnp.zeros((2, 8, 128), jnp.float32)
                return 0

            lax.fori_loop(0, HALO, go, 0)
            for part in range(2):
                ghost[part, side] = jnp.zeros((4, 128), jnp.float32)

        @pl.when(jnp.logical_not(has_low))
        def _():
            clear(0)

        @pl.when(jnp.logical_not(has_high))
        def _():
            clear(1)

        for copy in small:
            copy.wait()
        level_own = amp[phase[0]]
        jbuf[0, 0, 4:8, :] = jnp.full((4, 128), level_own, jnp.float32)

        spread_row = lax.broadcasted_iota(jnp.int32, (32, 128), 0)
        spread_col = lax.broadcasted_iota(jnp.int32, (32, 128), 1)
        spread = jnp.where(spread_row == (spread_col >> 2), 1.0, 0.0).astype(jnp.float32)
        quarter = lax.broadcasted_iota(jnp.int32, (4, 128), 0) == (
            lax.broadcasted_iota(jnp.int32, (4, 128), 1) & 3
        )
        rows = []
        for zc in range(4):
            wide = jnp.dot(
                rate[zc], spread, precision=lax.Precision.HIGHEST,
                preferred_element_type=jnp.float32,
            )
            rows.append(jnp.sum(jnp.where(quarter, wide, 0.0), axis=0, keepdims=True))
        packed_rate = jnp.concatenate(rows, axis=0)
        step_rate = packed_rate * (-1.0 / WINDOWS)
        decay = jnp.exp(step_rate)
        unclose = 1.0 / (1.0 - jnp.exp(-packed_rate))

        def powers(it):
            def go(i, _):
                dx, dy = i // 8, lax.rem(i, 8)
                lag = (xx - lax.rem(xx - dx + 4, 4)) * 8 + yy - lax.rem(yy - dy + 8, 8)
                for half in range(2):
                    power = lax.rem(lag - 2 * it + 32 * half + 2 * WINDOWS, WINDOWS)
                    weight[it, half, i] = jnp.exp(step_rate * power.astype(jnp.float32)) * unclose
                return 0

            lax.fori_loop(0, 32, go, 0, unroll=4)

        def lookup(m):
            picks = [cond[i] for i in range(16)]
            for bit in range(4):
                on = (m & (1 << bit)) != 0
                picks = [
                    jnp.where(on, picks[2 * i + 1], picks[2 * i])
                    for i in range(len(picks) // 2)
                ]
            return picks[0]

        level1 = level_own

        def arrange(lo, count, gain):
            def go(i, _):
                for half in range(2):
                    rows = pl.ds(half, 8, stride=2)
                    k = lo + i
                    u[k, half] = nat_u[k, rows, :]
                    c = lookup(nat_m[k, rows, :])
                    coef[k, half] = c if gain is None else c * gain
                    s = nat_s[k, rows, :]
                    src[k, half] = s
                    force[k, half] = level1 * s
                return 0

            lax.fori_loop(0, count, go, 0, unroll=2)

        for copy in locals_:
            copy.wait()
        pl.semaphore_wait(near, 4)
        tell(ring, tuple(plane_peer(dx, dy) for dx, dy in ((0, 2), (0, 6), (1, 0), (3, 0))))
        arrange(HALO, LAYERS, None)

        def slab_means():
            means = []
            for zc in range(4):
                base = HALO + 4 * zc
                means.append(
                    block_mean([u[base + i, half] for i in range(4) for half in range(2)])
                )
            return means

        start_mean = pack(slab_means())

        def advance(k, before, here, after):
            even, odd = here
            across = (
                odd + jnp.where(first_sub, zero, roll(odd, 1, 0)),
                even + jnp.where(last_sub, zero, roll(even, -1, 0)),
            )
            for half in range(2):
                now = here[half]
                total = before[half] + after[half] + across[half]
                total = total + jnp.where(first_lane, zero, roll(now, 1, 1))
                total = total + jnp.where(last_lane, zero, roll(now, -1, 1))
                u[k, half] = now + coef[k, half] * (total - 6.0 * now) + force[k, half]

        def layer(ref, k):
            return ref[k, 0], ref[k, 1]

        def sweep(base, lo, hi, below=None, above=None):
            before = below if below is not None else layer(u, base + lo - 1)
            here = layer(u, base + lo)
            for k in range(lo, hi):
                after = above if above is not None and k == hi - 1 else layer(u, base + k + 1)
                advance(base + k, before, here, after)
                before, here = here, after

        def inner():
            for t in range(1, 8):
                lo, hi = HALO + t, HALO + LAYERS - t
                for half in range(2):
                    low_edge[t, half] = u[lo, half]
                    high_edge[t, half] = u[hi - 1, half]
                sweep(0, lo, hi)

        def outer():
            for t in range(1, 8):
                sweep(0, t, HALO + t, above=layer(low_edge, t))
                sweep(0, EXT - HALO - t, EXT - t, below=layer(high_edge, t))

            def rest(i, _):
                sweep(0, 8, EXT - 8)
                return 0

            lax.fori_loop(0, 3, rest, 0)

        inner()
        pl.semaphore_wait(ring, 4)
        tell(cross, (plane_peer(0, 2), plane_peer(0, 6)))

        @pl.when(has_low)
        def _():
            for copy in halo_copies(1):
                copy.wait_recv()

        @pl.when(has_high)
        def _():
            for copy in halo_copies(0):
                copy.wait_recv()

        arrange(0, HALO, jnp.where(has_low, 1.0, 0.0))
        arrange(HALO + LAYERS, HALO, jnp.where(has_high, 1.0, 0.0))

        def pl_all(it, rows, sem):
            every = jbuf.at[it, pl.ds(1, 31), rows]
            return pltpu.make_async_copy(every, every, sem.at[it])

        def coarse_solve(it, jump, between):
            rows = pl.ds(0, 8 if it == 0 else 4)
            jbuf[it, 0, 0:4, :] = jump
            for dx, dy in peers:
                pltpu.make_async_remote_copy(
                    src_ref=jbuf.at[it, 0, rows], dst_ref=jbuf.at[it, 8 * dx + dy, rows],
                    send_sem=j_send.at[it], recv_sem=j_recv.at[it],
                    device_id=plane_peer(dx, dy), device_id_type=MESH,
                ).start()
            between()
            pl_all(it, rows, j_recv).wait()

            def weigh(half):
                terms = [weight[it, half, i] * jbuf[it, i, 0:4, :] for i in range(32)]
                while len(terms) > 1:
                    terms = [a + b for a, b in zip(terms[::2], terms[1::2])]
                return terms[0]

            ksend[it, 0:4, :] = weigh(1)
            if it == 0:
                ksend[0, 4:8, :] = jbuf[0, 31, 4:8, :]
            copy = pltpu.make_async_remote_copy(
                src_ref=ksend.at[it, rows], dst_ref=kbuf.at[it, rows],
                send_sem=k_send.at[it], recv_sem=k_recv.at[it],
                device_id=twin, device_id_type=MESH,
            )
            copy.start()
            if it == 0:
                ghost_step(0)
            total = weigh(0)
            if it == 0:
                tsend[...] = total
                ghost_step(1)
            copy.wait_recv()
            return total + kbuf[it, 0:4, :], [copy]

        def ghost_copy(part, side):
            target = (twin_tm if part == 0 else tm, slab - 1 if side == 0 else slab + 1)
            return pltpu.make_async_remote_copy(
                src_ref=ksend.at[0, pl.ds(0, 4)] if part == 0 else tsend,
                dst_ref=ghost.at[part, 1 - side],
                send_sem=g_send.at[part, side], recv_sem=g_recv.at[part, 1 - side],
                device_id=target, device_id_type=MESH,
            )

        def ghost_step(part):
            @pl.when(has_high)
            def _():
                ghost_copy(part, 1).start()

            @pl.when(has_low)
            def _():
                ghost_copy(part, 0).start()

        peers = sorted(
            [(dx, dy) for dx in range(4) for dy in range(8) if dx + dy > 0],
            key=lambda p: -min(p[0], 4 - p[0]) - min(p[1], 8 - p[1]),
        )
        pending = []
        outer()

        def detach():
            means = slab_means()
            for zc in range(4):
                for i in range(4):
                    k = HALO + 4 * zc + i
                    for half in range(2):
                        u[k, half] = u[k, half] - means[zc]
            return pack(means)

        end_mean = detach()
        jump = end_mean - decay * start_mean

        def halo2(side):
            peer = (tm, slab - 1) if side == 0 else (tm, slab + 1)
            rows = pl.ds(HALO, HALO) if side == 0 else pl.ds(LAYERS, HALO)
            return pltpu.make_async_remote_copy(
                src_ref=u.at[rows], dst_ref=dhalo.at[1 - side],
                send_sem=d_send.at[side], recv_sem=d_recv.at[side],
                device_id=peer, device_id_type=MESH,
            )

        def between1():
            @pl.when(has_high)
            def _():
                halo2(1).start()

            @pl.when(has_low)
            def _():
                halo2(0).start()

            powers(0)
            powers(1)

            @pl.when(zz == 0)
            def _():
                pl.semaphore_wait(up, 1)
                tell(up, (twin,))

            @pl.when(zz == 1)
            def _():
                pl.semaphore_wait(up, 1)

        pl.semaphore_wait(cross, 2)
        coarse, sends = coarse_solve(0, jump, between1)
        pending += sends

        @pl.when(has_high)
        def _():
            halo2(1).wait_send()

        @pl.when(has_low)
        def _():
            halo2(0).wait_send()

        for zc in range(4):
            wide = unpack(coarse[zc:zc + 1])
            for i in range(4):
                k = HALO + 4 * zc + i
                for half in range(2):
                    u[k, half] = u[k, half] + wide

        level2 = jnp.where(
            yy < 7, jbuf[0, 7, 4:5, :],
            jnp.where(xx < 3, jbuf[0, 31, 4:5, :], kbuf[0, 4:5, :]),
        )
        level2 = jnp.broadcast_to(level2, (8, 128))

        def reforce(k, _):
            for half in range(2):
                force[k, half] = level2 * src[k, half]
            return 0

        lax.fori_loop(0, EXT, reforce, 0, unroll=4)
        inner()

        @pl.when(has_low)
        def _():
            halo2(1).wait_recv()
            for part in range(2):
                ghost_copy(part, 1).wait_recv()

        @pl.when(has_high)
        def _():
            halo2(0).wait_recv()
            for part in range(2):
                ghost_copy(part, 0).wait_recv()

        low_wide = {r: unpack(ghost[0, 0, r:r + 1, :] + ghost[1, 0, r:r + 1, :]) for r in (1, 2, 3)}
        high_wide = {r: unpack(ghost[0, 1, r:r + 1, :] + ghost[1, 1, r:r + 1, :]) for r in (0, 1, 2)}
        for i in range(HALO):
            for half in range(2):
                u[i, half] = dhalo[0, i, half] + low_wide[(LAYERS - HALO + i) // 4]
                u[HALO + LAYERS + i, half] = dhalo[1, i, half] + high_wide[i // 4]

        outer()

        end_mean = detach()
        jump = end_mean - decay * coarse
        final_copy = pltpu.make_async_remote_copy(
            src_ref=u.at[own], dst_ref=fin, send_sem=f_send, recv_sem=f_recv,
            device_id=(last, slab), device_id_type=MESH,
        )
        coarse, sends = coarse_solve(1, jump, final_copy.start)
        pending += sends
        wides = [unpack(coarse[zc:zc + 1]) for zc in range(4)]
        def result_copy(zc):
            part = pl.ds(4 * zc, 4)
            return pltpu.make_async_copy(result.at[part], out.at[0, part], f_out.at[zc])

        final_copy.wait_recv()
        for zc in range(4):
            for i in range(4):
                k = 4 * zc + i
                for half in range(2):
                    result[k, pl.ds(half, 8, stride=2), :] = fin[k, half] + wides[zc]
            result_copy(zc).start()

        for copy in pending:
            copy.wait_send()
        pl_all(0, pl.ds(0, 8), j_send).wait()
        pl_all(1, pl.ds(0, 4), j_send).wait()
        final_copy.wait_send()
        for zc in range(4):
            result_copy(zc).wait()

        @pl.when(has_high)
        def _():
            for copy in halo_copies(1):
                copy.wait_send()
            for part in range(2):
                ghost_copy(part, 1).wait_send()

        @pl.when(has_low)
        def _():
            for copy in halo_copies(0):
                copy.wait_send()
            for part in range(2):
                ghost_copy(part, 0).wait_send()

    return kernel


def body(start_states, material, source, conductivity, tide_amp, phase, coarse_rate):
    f32 = jnp.float32
    hbm = pl.BlockSpec(memory_space=pltpu.HBM)
    somewhere = pl.BlockSpec(memory_space=pl.ANY)
    dma = pltpu.SemaphoreType.DMA
    regular = pltpu.SemaphoreType.REGULAR
    field = pltpu.VMEM((EXT, 2, 8, 128), f32)
    return pl.pallas_call(
        make_kernel(),
        out_shape=jax.ShapeDtypeStruct((1, LAYERS, 16, 128), f32),
        in_specs=[hbm] * 7,
        out_specs=somewhere,
        scratch_shapes=[
            pltpu.SMEM((16,), f32),
            pltpu.SMEM((12,), f32),
            pltpu.SMEM((1,), jnp.int32),
            pltpu.VMEM((4, 4, 32), f32),
            pltpu.VMEM((LAYERS, 16, 128), f32),
            pltpu.VMEM((8, 2, 8, 128), f32),
            pltpu.VMEM((8, 2, 8, 128), f32),
            pltpu.VMEM((EXT, 16, 128), f32),
            pltpu.VMEM((EXT, 16, 128), jnp.int32),
            pltpu.VMEM((EXT, 16, 128), f32),
            field, field, field, field,
            pltpu.VMEM((2, 32, 8, 128), f32),
            pltpu.VMEM((2, 8, 128), f32),
            pltpu.VMEM((2, 8, 128), f32),
            pltpu.VMEM((4, 128), f32),
            pltpu.VMEM((2, 2, 4, 128), f32),
            pltpu.VMEM((2, 2, 32, 4, 128), f32),
            pltpu.VMEM((2, HALO, 2, 8, 128), f32),
            pltpu.VMEM((LAYERS, 2, 8, 128), f32),
            dma((7,)), dma((2, 3)), dma((2, 3)),
            dma((2,)), dma((2,)), dma((2,)), dma((2,)),
            dma((2,)), dma((2,)), dma((2, 2)), dma((2, 2)),
            dma(()), dma(()), dma((4,)), regular, regular, regular, regular,
        ],
        compiler_params=pltpu.CompilerParams(
            collective_id=0, has_side_effects=True, vmem_limit_bytes=VMEM_BYTES
        ),
    )(
        *(
            pltpu.with_memory_space_constraint(x, pltpu.HBM)
            for x in (start_states, material, source, conductivity, tide_amp)
        ),
        phase,
        pltpu.with_memory_space_constraint(coarse_rate, pltpu.HBM),
    )


def solution(mesh):
    placed = (
        P("tm", "space", None, None),
        P("space", None, None),
        P("space", None, None),
        P(),
        P(),
        P("tm"),
        P("space", None, None),
    )
    return jax.shard_map(
        body, mesh=mesh, in_specs=placed, out_specs=P("tm", "space", None, None), check_vma=False
    )
```
